32 devices in a mesh: freq: 4 (over z), cell: 8 (over y, x, core).
Axes of the slice: x: 2, y: 2, z: 4, core: 2. Of those that a mesh axis runs over, the one named last changes fastest.
Arguments:
- green: bfloat16 [2, 8, 1024, 4096], P(None, 'freq', None, 'cell'), may hold values from -0.25 to 0.25
- coeffs: float32 [8, 4096], P('freq', 'cell'), may hold values from -6 to 6
- basis: float32 [8, 8], P('freq'), may hold values from -2 to 2
- amplitude: float32 [8, 1024], P('freq'), may hold values from 0.5 to 2
- block_mask: int32 [16, 16], replicated, may hold values 0 or 1
Outputs:
- hess_vec: float32 [8, 4096], P('freq', 'cell')
The draws below stay inside these ranges and needn't reach their ends.
All inputs are finite; a program needn't handle non-finite values.
Results may differ from the reference program's by a relative error of at most 0.0024.
Values may be sent and summed in bfloat16 or wider, within the bound.
No kernel may reach another device: no remote copies, remote signals or barrier semaphores. Data moves between devices by JAX's collectives and lax.ppermute only.
A program may use at most 192 MiB of HBM per device.

```python
import math
import jax
import jax.numpy as jnp
from jax import lax

NS = 1024
SB = 64
NB = 8
CELL_DEV = 512
NF = 8
NC = 4096
NSB = 16
N_CELL = 8


def place_ends(result, key, low, largest):
    longest = result.shape.index(max(result.shape))
    spots = []
    for shift in (0, 1):
        where = [jax.random.randint(jax.random.fold_in(key, axis), (), 0, length) for axis, length in enumerate(result.shape)]
        where[longest] = (where[longest] + shift) % result.shape[longest]
        spots.append(tuple(where))
    return result.at[spots[0]].set(low).at[spots[1]].set(largest)


def raised(drawn, rng, source, target, shards_of, factor):
    owner, partner = [(jnp.arange(drawn.shape[dim]) // (drawn.shape[dim] // shards_of)).reshape([-1 if axis == dim else 1 for axis in range(drawn.ndim)]) for dim in (source, target)]
    chosen = jax.random.permutation(rng, shards_of)[partner]
    strong = (owner == chosen) | (owner == (partner + shards_of // 2) % shards_of)
    return jnp.where(strong, factor * drawn, drawn)


def level_of(stream_key, shape, pieces, least, high):
    def one(position, blocks):
        draws = jax.random.uniform(jax.random.fold_in(jax.random.fold_in(stream_key, 6), position), (blocks,), jnp.float32, least / len(pieces), high / len(pieces))
        return jnp.repeat(jnp.exp(draws), shape[position] // blocks).reshape((-1,) + (1,) * (len(shape) - position - 1))

    loudness = one(*pieces[0])
    for cut in pieces[1:]:
        loudness = loudness * one(*cut)
    return loudness


def scatter_about(rng, extent, scale, reach, pieces=(), held_as=jnp.bfloat16):
    level = level_of(rng, extent, pieces, -0.22, 0.18) if pieces else 1.0
    result = jax.random.normal(rng, extent, jnp.float32) * scale * level
    return jnp.minimum(jnp.maximum(result, -reach), reach).astype(held_as)


def bell_draw_with(own_key, shape, spread, limit, shards, heavy, held_as=jnp.bfloat16):
    entries = spread * jax.random.normal(own_key, shape, jnp.float32)
    if shards:
        entries = entries * level_of(own_key, shape, shards, -0.22, 0.18)
    return jnp.clip(raised(entries, jax.random.fold_in(own_key, 3), *heavy), -limit, limit).astype(held_as)


def setup_inputs(seed: int = 0) -> dict:
    key_list = jax.random.split(jax.random.key(seed), 6)
    return {
        "green": bell_draw_with(key_list[0], (2, NF, NS, NC), NS ** -0.5, 0.25, ((1, 4), (3, 8)), (3, 2, 8, 2.0)),
        "coeffs": scatter_about(key_list[1], (NB, NC), 1.0, 6.0, ((0, 4), (1, 8)), jnp.float32),
        "basis": scatter_about(key_list[2], (NF, NB), NB ** -0.5, 2.0, ((0, 4),), jnp.float32),
        "amplitude": jnp.clip(jnp.exp(math.log(2.0) - 1.3862944 * jax.random.uniform(key_list[3], (NF, NS), jnp.float32) ** level_of(key_list[3], (NF, NS), ((0, 4),), -0.2, 0.2)), 0.5, 2.0),
        "block_mask": place_ends((jax.random.randint(key_list[4], (NSB, NSB), 0, 4) < 3).astype(jnp.int32), jax.random.fold_in(key_list[4], 1), 0, 1),
    }


def reference(green, coeffs, basis, amplitude, block_mask):
    highest = lax.Precision.HIGHEST
    source = jnp.dot(basis, coeffs, precision=highest)
    scaled = (green.astype(jnp.float32) * source[None, :, None, :]).astype(jnp.bfloat16)

    def one_block(total, index):
        start = (index * CELL_DEV).astype(jnp.int32)
        left = lax.dynamic_slice_in_dim(scaled, start, CELL_DEV, 3).astype(jnp.float32)
        local = lax.dynamic_slice_in_dim(green, start, CELL_DEV, 3).astype(jnp.float32)
        right = jnp.stack((jnp.stack((local[0], local[1])), jnp.stack((-local[1], local[0]))))
        term = jnp.einsum("pfic,qpfjc->fqij", left, right)
        rounded = lax.optimization_barrier(term.astype(jnp.bfloat16))
        return total + rounded.astype(jnp.float32), None

    empty = jnp.zeros((NF, 2, NS, NS), jnp.float32)
    corr, _ = lax.scan(one_block, empty, jnp.arange(N_CELL, dtype=jnp.int32))
    expanded = jnp.broadcast_to(block_mask[:, None, :, None], (NSB, SB, NSB, SB)).reshape(NS, NS).astype(jnp.float32)
    weight = amplitude[:, :, None] * amplitude[:, None, :] * expanded[None]
    resid = (weight[:, None] * corr).astype(jnp.bfloat16)

    def sense(pair):
        rows, field = pair
        rf = rows.astype(jnp.float32)
        gf = field.astype(jnp.float32)
        yre = jnp.dot(rf[0], gf[0], preferred_element_type=jnp.float32) - jnp.dot(rf[1], gf[1], preferred_element_type=jnp.float32)
        yim = jnp.dot(rf[0], gf[1], preferred_element_type=jnp.float32) + jnp.dot(rf[1], gf[0], preferred_element_type=jnp.float32)
        return jnp.sum(gf[0] * yre + gf[1] * yim, axis=0)

    sens = lax.map(sense, (resid, jnp.moveaxis(green, 1, 0)))
    return jnp.dot(basis.T, sens, precision=highest)
```

```python
import functools

import jax
import jax.numpy as jnp
from jax import lax
from jax.experimental import pallas as pl
from jax.experimental.pallas import tpu as pltpu
from jax.sharding import PartitionSpec as P

F32 = jnp.float32
BF16 = jnp.bfloat16
MIB = 1 << 20


def across(left, right):
    return lax.dot_general(left, right, (((1,), (1,)), ((), ())), preferred_element_type=F32)


def along(left, right):
    return jnp.dot(left, right, preferred_element_type=F32)


def corr_kernel(n, piece_ref, source_ref, green_ref, out_ref):
    stations, width = green_ref.shape
    tile, half = stations // n, width // 2
    piece = piece_ref[0]

    def block(d):
        start = lax.rem(piece + d, n) * tile
        return green_ref[pl.ds(pl.multiple_of(start, tile), tile), :]

    scaled = (block(0).astype(F32) * source_ref[...]).astype(BF16)
    turned = jnp.concatenate((scaled[:, half:], -scaled[:, :half]), axis=1)
    both = jnp.concatenate((scaled, turned), axis=0)
    pair = across(both, block(0))
    row = lax.broadcasted_iota(jnp.int32, (tile, tile), 0)
    col = lax.broadcasted_iota(jnp.int32, (tile, tile), 1)
    out_ref[:, :tile] = jnp.where(row >= col, pair[:tile], pair[tile:]).astype(out_ref.dtype)
    for d in range(1, n // 2):
        pair = across(both, block(d)).astype(out_ref.dtype)
        out_ref[:, (2 * d - 1) * tile : 2 * d * tile] = pair[:tile]
        out_ref[:, 2 * d * tile : (2 * d + 1) * tile] = pair[tile:]
    last = across(jnp.where(piece < n // 2, scaled, turned), block(n // 2))
    out_ref[:, (n - 1) * tile :] = last.astype(out_ref.dtype)


def sens_kernel(n, step, piece_ref, resid_ref, green_ref, out_ref):
    stations, width = green_ref.shape
    tile, half = stations // n, width // 2
    piece = piece_ref[0]
    starts = [pl.multiple_of(lax.rem(piece + d, n) * tile, tile) for d in range(n // 2 + 1)]
    row = lax.broadcasted_iota(jnp.int32, (tile, tile), 0)
    col = lax.broadcasted_iota(jnp.int32, (tile, tile), 1)
    diag = resid_ref[:, :tile].astype(F32)
    lower = jnp.where(row > col, diag, jnp.where(row == col, 0.5 * diag, 0.0)).astype(BF16)
    upper = jnp.where(row < col, diag, 0.0).astype(BF16)
    last = resid_ref[:, (n - 1) * tile :]
    real = piece < n // 2
    for at in range(0, half, step):

        def fields(d):
            rows = pl.ds(starts[d], tile)
            return green_ref[rows, at : at + step], green_ref[rows, half + at : half + at + step]

        re_here, im_here = fields(0)
        pu, pv = along(lower, re_here), along(lower, im_here)
        qu, qv = along(upper, re_here), along(upper, im_here)
        for d in range(1, n // 2):
            re, im = fields(d)
            p = resid_ref[:, (2 * d - 1) * tile : 2 * d * tile]
            q = resid_ref[:, 2 * d * tile : (2 * d + 1) * tile]
            pu, pv = pu + along(p, re), pv + along(p, im)
            qu, qv = qu + along(q, re), qv + along(q, im)
        re, im = fields(n // 2)
        hu, hv = along(last, re), along(last, im)
        yre = pu - qv + jnp.where(real, hu, -hv)
        yim = pv + qu + jnp.where(real, hv, hu)
        share = re_here.astype(F32) * yre + im_here.astype(F32) * yim
        out_ref[:, at : at + step] = 2.0 * jnp.sum(share, axis=0, keepdims=True)


SMEM = pl.BlockSpec(memory_space=pltpu.SMEM)
VMEM = pl.BlockSpec(memory_space=pltpu.VMEM)


def corr_piece(n, piece, source, green, dtype):
    stations, width = green.shape
    tile = stations // n
    return pl.pallas_call(
        functools.partial(corr_kernel, n),
        out_shape=jax.ShapeDtypeStruct((tile, stations), dtype),
        in_specs=[SMEM, VMEM, VMEM],
        out_specs=VMEM,
        compiler_params=pltpu.CompilerParams(vmem_limit_bytes=24 * MIB),
        cost_estimate=pl.CostEstimate(
            flops=2 * tile * stations * width * 5 // 4,
            bytes_accessed=2 * stations * width + 4 * tile * stations,
            transcendentals=0,
        ),
        name="corr_piece",
    )(piece, source, green)


def sens_piece(n, piece, resid, green):
    stations, width = green.shape
    tile = stations // n
    return pl.pallas_call(
        functools.partial(sens_kernel, n, min(512, width // 2)),
        out_shape=jax.ShapeDtypeStruct((1, width // 2), F32),
        in_specs=[SMEM, VMEM, VMEM],
        out_specs=VMEM,
        compiler_params=pltpu.CompilerParams(vmem_limit_bytes=24 * MIB),
        cost_estimate=pl.CostEstimate(
            flops=2 * tile * stations * width * 5 // 4,
            bytes_accessed=2 * stations * width + 2 * tile * stations,
            transcendentals=0,
        ),
        name="sens_piece",
    )(piece, resid, green)


def on_device(n_freq, n_cell, green, coeffs, basis, amplitude, block_mask):
    n = n_cell // 2
    bits, z_bits = n.bit_length() - 1, n_freq.bit_length() - 1
    stations, cells = green.shape[2], green.shape[3]
    tile = stations // n
    here = lax.axis_index("cell")
    core, chip, plane = here % 2, here // 2, lax.axis_index("freq")

    def dims(which):
        return [(which + j) % bits for j in range(bits)]

    swap_core = [(i, i ^ 1) for i in range(n_cell)]

    def swap_chip(value, j):
        pairs = [(i, i ^ (2 << dims(i % 2)[j])) for i in range(n_cell)]
        return lax.ppermute(value, "cell", pairs)

    def swap_plane(value, j):
        return lax.ppermute(value, "freq", [(i, i ^ (1 << j)) for i in range(n_freq)])

    def piece_of(q):
        flips = [sum(((q >> j) & 1) << dims(which)[j] for j in range(bits)) for which in (0, 1)]
        return (chip ^ jnp.where(core == 0, flips[0], flips[1])).astype(jnp.int32).reshape(1)

    known = jnp.concatenate((coeffs, lax.ppermute(coeffs, "cell", swap_core)), axis=1)
    for j in range(z_bits):
        known = jnp.concatenate((known, swap_plane(known, j)), axis=0)
    order = plane ^ jnp.arange(n_freq)
    basis_near = basis.reshape(2, n_freq, -1)[:, order].reshape(2, -1)
    basis_mine = lax.dynamic_index_in_dim(basis_near, core, 0, keepdims=False)
    basis_other = lax.dynamic_index_in_dim(basis_near, 1 - core, 0, keepdims=False)
    source = jnp.sum(basis_mine[:, None] * known, axis=0, keepdims=True)
    source = jnp.concatenate((source, source), axis=1)

    mine = lax.dynamic_index_in_dim(green, core, 1, keepdims=False)
    theirs = lax.ppermute(
        lax.dynamic_index_in_dim(green, 1 - core, 1, keepdims=False), "cell", swap_core
    )
    field = jnp.concatenate((mine[0], theirs[0], mine[1], theirs[1]), axis=1)

    own = piece_of(0)[0]
    columns = [0] + [d for d in range(1, n // 2) for _ in (0, 1)] + [n // 2]
    amp = lax.dynamic_index_in_dim(amplitude, core, 0, keepdims=False).reshape(n, tile)
    col_blocks = (own + jnp.array(columns)) % n
    amp_rows, amp_cols = amp[own], amp[col_blocks].reshape(-1)
    n_blocks = block_mask.shape[0]
    size = stations // n_blocks
    symmetric = (0.5 * (block_mask + block_mask.T)).astype(BF16)
    inside = jnp.arange(tile)
    row_block = (own * tile + inside) // size
    col_block = ((col_blocks * tile)[:, None] + inside[None, :]).reshape(-1) // size
    numbers = jnp.arange(n_blocks)
    pick_rows = (row_block[:, None] == numbers[None, :]).astype(BF16)
    pick_cols = (numbers[:, None] == col_block[None, :]).astype(BF16)
    spread = along(along(pick_rows, symmetric).astype(BF16), pick_cols)
    weight = amp_rows[:, None] * amp_cols[None, :] * spread

    held = {}
    first = sorted((q for q in range(n) if q & 1), reverse=True)
    for q in first + sorted((q for q in range(n) if not q & 1), reverse=True):
        held[q] = corr_piece(n, piece_of(q), source, field, BF16 if q & 1 else F32)
    for j in range(bits):
        for q in sorted((q for q in held if (q >> j) & 1), reverse=True):
            got = swap_chip(held.pop(q).astype(BF16), j)
            rest = q ^ (1 << j)
            held[rest] = held[rest] + got.astype(F32)
    resid = {0: (held[0] * weight).astype(BF16)}

    for j in reversed(range(bits)):
        for q in sorted(resid):
            resid[q | (1 << j)] = swap_chip(resid[q], j)
    sens = sum(sens_piece(n, piece_of(q), resid[q], field) for q in resid)

    other = lax.ppermute(sens[:, cells:], "cell", swap_core)
    partial = basis_mine[:, None] * sens[:, :cells] + basis_other[:, None] * other
    for j in reversed(range(z_bits)):
        middle = partial.shape[0] // 2
        partial = partial[:middle] + swap_plane(partial[middle:], j)
    return partial


def solution(mesh):
    placed = (
        P(None, "freq", None, "cell"),
        P("freq", "cell"),
        P("freq", None),
        P("freq", None),
        P(),
    )
    n_freq, n_cell = mesh.shape["freq"], mesh.shape["cell"]
    return jax.shard_map(
        functools.partial(on_device, n_freq, n_cell),
        mesh=mesh,
        in_specs=placed,
        out_specs=P("freq", "cell"),
        check_vma=False,
    )
```

```python
import functools

import jax
import jax.numpy as jnp
from jax import lax
from jax.experimental import pallas as pl
from jax.experimental.pallas import tpu as pltpu
from jax.sharding import PartitionSpec as P

F32 = jnp.float32
BF16 = jnp.bfloat16
MIB = 1 << 20


def across(left, right):
    return lax.dot_general(left, right, (((1,), (1,)), ((), ())), preferred_element_type=F32)


def along(left, right):
    return jnp.dot(left, right, preferred_element_type=F32)


def copy_all(sems, pairs):
    copies = [pltpu.make_async_copy(src, dst, sems.at[i]) for i, (src, dst) in enumerate(pairs)]
    for copy in copies:
        copy.start()
    for copy in copies:
        copy.wait()


def take_kernel(core_ref, green_ref, out_ref, sems):
    other = 1 - core_ref[0]
    copy_all(sems, [(green_ref.at[p, other], out_ref.at[p]) for p in (0, 1)])


def field_kernel(core_ref, green_ref, theirs_ref, out_ref, sems):
    core, cells = core_ref[0], green_ref.shape[3]
    pairs = []
    for p in (0, 1):
        pairs.append((green_ref.at[p, core], out_ref.at[:, pl.ds(2 * p * cells, cells)]))
        pairs.append((theirs_ref.at[p], out_ref.at[:, pl.ds((2 * p + 1) * cells, cells)]))
    copy_all(sems, pairs)


def weight_kernel(n, place_ref, amp_ref, mask_ref, out_ref):
    core, piece = place_ref[0], place_ref[1]
    tile, stations = out_ref.shape
    blocks = mask_ref.shape[0]
    size = stations // blocks

    def amp(start):
        both = amp_ref[:, pl.ds(pl.multiple_of(start, tile), tile)]
        return jnp.where(core == 0, both[0:1], both[1:2])

    here = piece * tile
    row = lax.broadcasted_iota(jnp.int32, (tile, tile), 0)
    col = lax.broadcasted_iota(jnp.int32, (tile, tile), 1)
    down = jnp.sum(jnp.where(row == col, amp(here), 0.0), axis=1, keepdims=True)
    mask = mask_ref[...].astype(BF16)
    low = lax.broadcasted_iota(jnp.int32, (tile, blocks), 1) * size
    at = here + lax.broadcasted_iota(jnp.int32, (tile, blocks), 0)
    pick = ((at >= low) & (at < low + size)).astype(BF16)
    rows = (0.5 * (along(pick, mask) + across(pick, mask))).astype(BF16)
    low = lax.broadcasted_iota(jnp.int32, (blocks, tile), 0) * size
    for d in range(n // 2 + 1):
        start = lax.rem(piece + d, n) * tile
        at = start + lax.broadcasted_iota(jnp.int32, (blocks, tile), 1)
        pick = ((at >= low) & (at < low + size)).astype(BF16)
        weight = down * amp(start) * along(rows, pick)
        for i in ([0] if d == 0 else [2 * d - 1] if d == n // 2 else [2 * d - 1, 2 * d]):
            out_ref[:, i * tile : (i + 1) * tile] = weight


def corr_kernel(n, place_ref, basis_ref, known_ref, green_ref, out_ref):
    stations, width = green_ref.shape
    tile, half = stations // n, width // 2
    core, plane, piece = place_ref[0], place_ref[1], place_ref[2]

    def block(d):
        start = lax.rem(piece + d, n) * tile
        return green_ref[pl.ds(pl.multiple_of(start, tile), tile), :]

    planes, each = known_ref.shape[0], known_ref.shape[1]
    source = jnp.zeros((1, half), F32)
    for r in range(planes):
        for k in range(each):
            source = source + basis_ref[core, (plane ^ r) * each + k] * known_ref[r, k : k + 1, :]
    source = jnp.concatenate((source, source), axis=1)
    scaled = (block(0).astype(F32) * source).astype(BF16)
    turned = jnp.concatenate((scaled[:, half:], -scaled[:, :half]), axis=1)
    both = jnp.concatenate((scaled, turned), axis=0)
    pair = across(both, block(0))
    row = lax.broadcasted_iota(jnp.int32, (tile, tile), 0)
    col = lax.broadcasted_iota(jnp.int32, (tile, tile), 1)
    out_ref[:, :tile] = jnp.where(row >= col, pair[:tile], pair[tile:]).astype(out_ref.dtype)
    for d in range(1, n // 2):
        pair = across(both, block(d)).astype(out_ref.dtype)
        out_ref[:, (2 * d - 1) * tile : 2 * d * tile] = pair[:tile]
        out_ref[:, 2 * d * tile : (2 * d + 1) * tile] = pair[tile:]
    last = across(jnp.where(piece < n // 2, scaled, turned), block(n // 2))
    out_ref[:, (n - 1) * tile :] = last.astype(out_ref.dtype)


def sens_kernel(n, step, piece_ref, resid_ref, green_ref, out_ref):
    stations, width = green_ref.shape
    tile, half = stations // n, width // 2
    piece = piece_ref[0]
    starts = [pl.multiple_of(lax.rem(piece + d, n) * tile, tile) for d in range(n // 2 + 1)]
    row = lax.broadcasted_iota(jnp.int32, (tile, tile), 0)
    col = lax.broadcasted_iota(jnp.int32, (tile, tile), 1)
    diag = resid_ref[:, :tile].astype(F32)
    lower = jnp.where(row > col, diag, jnp.where(row == col, 0.5 * diag, 0.0)).astype(BF16)
    upper = jnp.where(row < col, diag, 0.0).astype(BF16)
    last = resid_ref[:, (n - 1) * tile :]
    real = piece < n // 2
    for at in range(0, half, step):

        def fields(d):
            rows = pl.ds(starts[d], tile)
            return green_ref[rows, at : at + step], green_ref[rows, half + at : half + at + step]

        re_here, im_here = fields(0)
        pu, pv = along(lower, re_here), along(lower, im_here)
        qu, qv = along(upper, re_here), along(upper, im_here)
        for d in range(1, n // 2):
            re, im = fields(d)
            p = resid_ref[:, (2 * d - 1) * tile : 2 * d * tile]
            q = resid_ref[:, 2 * d * tile : (2 * d + 1) * tile]
            pu, pv = pu + along(p, re), pv + along(p, im)
            qu, qv = qu + along(q, re), qv + along(q, im)
        re, im = fields(n // 2)
        hu, hv = along(last, re), along(last, im)
        yre = pu - qv + jnp.where(real, hu, -hv)
        yim = pv + qu + jnp.where(real, hv, hu)
        share = re_here.astype(F32) * yre + im_here.astype(F32) * yim
        out_ref[:, at : at + step] = 2.0 * jnp.sum(share, axis=0, keepdims=True)


def hess_kernel(planes, place_ref, basis_ref, sens_ref, other_ref, out_ref):
    core, plane = place_ref[0], place_ref[1]
    each = out_ref.shape[0] // planes
    mine, other = sens_ref[:, : out_ref.shape[1]], other_ref[...]
    for r in range(planes):
        for k in range(each):
            b, i = (plane ^ r) * each + k, r * each + k
            out_ref[i : i + 1, :] = basis_ref[core, b] * mine + basis_ref[1 - core, b] * other


SMEM = pl.BlockSpec(memory_space=pltpu.SMEM)
VMEM = pl.BlockSpec(memory_space=pltpu.VMEM)
HBM = pl.BlockSpec(memory_space=pltpu.HBM)


def call(kernel, name, shape, dtype, specs, flops, moved, grant, *args, scratch=()):
    return pl.pallas_call(
        kernel,
        out_shape=jax.ShapeDtypeStruct(shape, dtype),
        in_specs=specs,
        out_specs=VMEM,
        scratch_shapes=scratch,
        compiler_params=pltpu.CompilerParams(vmem_limit_bytes=grant * MIB),
        cost_estimate=pl.CostEstimate(flops=flops, bytes_accessed=moved, transcendentals=0),
        name=name,
    )(*args)


def on_device(n_freq, n_cell, green, coeffs, basis, amplitude, block_mask):
    n = n_cell // 2
    bits, z_bits = n.bit_length() - 1, n_freq.bit_length() - 1
    stations, cells = green.shape[2], green.shape[3]
    tile, width, each = stations // n, 4 * cells, coeffs.shape[0]
    here = lax.axis_index("cell").astype(jnp.int32)
    plane = lax.axis_index("freq").astype(jnp.int32)
    core, chip = here % 2, here // 2
    flops = 2 * tile * stations * width * 5 // 4
    moved = 2 * stations * width + 2 * tile * stations

    def dims(which):
        return [(which + j) % bits for j in range(bits)]

    swap_core = [(i, i ^ 1) for i in range(n_cell)]

    def swap_chip(value, j):
        pairs = [(i, i ^ (2 << dims(i % 2)[j])) for i in range(n_cell)]
        return lax.ppermute(value, "cell", pairs)

    def swap_plane(value, j):
        return lax.ppermute(value, "freq", [(i, i ^ (1 << j)) for i in range(n_freq)])

    def piece_of(q):
        flips = [sum(((q >> j) & 1) << dims(which)[j] for j in range(bits)) for which in (0, 1)]
        return chip ^ jnp.where(core == 0, flips[0], flips[1])

    beside = lax.ppermute(coeffs, "cell", swap_core)
    core_only = core.reshape(1)
    two = [pltpu.SemaphoreType.DMA((2,))]
    theirs = call(
        take_kernel, "take", (2, stations, cells), BF16, [SMEM, HBM], 0,
        8 * stations * cells, 59, core_only, green, scratch=two,
    )
    theirs = lax.ppermute(theirs, "cell", swap_core)
    known = jnp.concatenate((coeffs, beside), axis=1)[None]
    for j in range(z_bits):
        known = jnp.concatenate((known, swap_plane(known, j)), axis=0)

    field = call(
        field_kernel, "field", (stations, width), BF16, [SMEM, HBM, HBM], 0,
        4 * stations * width, 56, core_only, green, theirs, scratch=[pltpu.SemaphoreType.DMA((4,))],
    )

    def corr_piece(q):
        return call(
            functools.partial(corr_kernel, n), "corr", (tile, stations), F32 if q % 2 == 0 else BF16,
            [SMEM, SMEM, VMEM, VMEM], flops, moved, 24,
            jnp.stack((core, plane, piece_of(q))), basis, known, field,
        )

    held = {}
    for q in sorted(range(n), key=lambda q: (q % 2 == 0, -q)):
        held[q] = corr_piece(q)
    weight = call(
        functools.partial(weight_kernel, n), "weight", (tile, stations), F32, [SMEM, VMEM, VMEM],
        0, 4 * tile * stations, 8, jnp.stack((core, piece_of(0))), amplitude, block_mask,
    )
    for j in range(bits):
        for q in sorted((q for q in held if (q >> j) & 1), reverse=True):
            got = swap_chip(held.pop(q).astype(BF16), j)
            rest = q ^ (1 << j)
            held[rest] = held[rest] + got.astype(F32)
    resid = {0: (held[0] * weight).astype(BF16)}

    def sens_piece(q):
        return call(
            functools.partial(sens_kernel, n, min(512, width // 2)), "sens", (1, width // 2), F32,
            [SMEM, VMEM, VMEM], flops, moved, 24, piece_of(q).reshape(1), resid[q], field,
        )

    sens = {}
    for j in reversed(range(bits)):
        for q in sorted(resid):
            if q == 0 and 0 in sens:
                sent, sens[0] = lax.optimization_barrier((resid[0], sens[0]))
            else:
                sent = resid[q]
            resid[q | (1 << j)] = swap_chip(sent, j)
            if 0 not in sens:
                sens[0] = sens_piece(0)
    for q in sorted(resid):
        if q not in sens:
            sens[q] = sens_piece(q)
    total = sum(sens.values())

    other = lax.ppermute(total[:, cells:], "cell", swap_core)
    partial = call(
        functools.partial(hess_kernel, n_freq), "hess", (n_freq * each, cells), F32,
        [SMEM, SMEM, VMEM, VMEM], 0, 4 * n_freq * each * cells, 4,
        jnp.stack((core, plane)), basis, total, other,
    )
    for j in reversed(range(z_bits)):
        middle = partial.shape[0] // 2
        partial = partial[:middle] + swap_plane(partial[middle:], j)
    return partial


def solution(mesh):
    placed = (
        P(None, "freq", None, "cell"),
        P("freq", "cell"),
        P("freq", None),
        P("freq", None),
        P(),
    )
    n_freq, n_cell = mesh.shape["freq"], mesh.shape["cell"]
    return jax.shard_map(
        functools.partial(on_device, n_freq, n_cell),
        mesh=mesh,
        in_specs=placed,
        out_specs=P("freq", "cell"),
        check_vma=False,
    )
```

```python
import functools

import jax
import jax.numpy as jnp
from jax import lax
from jax.experimental import pallas as pl
from jax.experimental.pallas import tpu as pltpu
from jax.sharding import PartitionSpec as P


F32 = jnp.float32
BF16 = jnp.bfloat16
MIB = 1 << 20


def across(left, right):
    return lax.dot_general(left, right, (((1,), (1,)), ((), ())), preferred_element_type=F32)


def along(left, right):
    return jnp.dot(left, right, preferred_element_type=F32)


def copy_all(sems, pairs):
    copies = [pltpu.make_async_copy(src, dst, sems.at[i]) for i, (src, dst) in enumerate(pairs)]
    for copy in copies:
        copy.start()
    for copy in copies:
        copy.wait()


def take_kernel(core_ref, green_ref, out_ref, sems):
    other = 1 - core_ref[0]
    copy_all(sems, [(green_ref.at[p, other], out_ref.at[p]) for p in (0, 1)])


def field_kernel(core_ref, green_ref, theirs_ref, out_ref, sems):
    core, cells = core_ref[0], green_ref.shape[3]
    pairs = []
    for p in (0, 1):
        pairs.append((green_ref.at[p, core], out_ref.at[:, pl.ds(2 * p * cells, cells)]))
        pairs.append((theirs_ref.at[p], out_ref.at[:, pl.ds((2 * p + 1) * cells, cells)]))
    copy_all(sems, pairs)


def weight_kernel(n, place_ref, amp_ref, mask_ref, out_ref):
    core, piece = place_ref[0], place_ref[1]
    tile, stations = out_ref.shape
    blocks = mask_ref.shape[0]
    size = stations // blocks

    def amp(start):
        both = amp_ref[:, pl.ds(pl.multiple_of(start, tile), tile)]
        return jnp.where(core == 0, both[0:1], both[1:2])

    here = piece * tile
    row = lax.broadcasted_iota(jnp.int32, (tile, tile), 0)
    col = lax.broadcasted_iota(jnp.int32, (tile, tile), 1)
    down = jnp.sum(jnp.where(row == col, amp(here), 0.0), axis=1, keepdims=True)
    mask = mask_ref[...].astype(BF16)
    low = lax.broadcasted_iota(jnp.int32, (tile, blocks), 1) * size
    at = here + lax.broadcasted_iota(jnp.int32, (tile, blocks), 0)
    pick = ((at >= low) & (at < low + size)).astype(BF16)
    rows = (0.5 * (along(pick, mask) + across(pick, mask))).astype(BF16)
    low = lax.broadcasted_iota(jnp.int32, (blocks, tile), 0) * size
    for d in range(n // 2 + 1):
        start = lax.rem(piece + d, n) * tile
        at = start + lax.broadcasted_iota(jnp.int32, (blocks, tile), 1)
        pick = ((at >= low) & (at < low + size)).astype(BF16)
        weight = down * amp(start) * along(rows, pick)
        for i in ([0] if d == 0 else [2 * d - 1] if d == n // 2 else [2 * d - 1, 2 * d]):
            out_ref[:, i * tile : (i + 1) * tile] = weight


def corr_kernel(n, place_ref, basis_ref, known_ref, green_ref, out_ref):
    stations, width = green_ref.shape
    tile, half = stations // n, width // 2
    core, plane, piece = place_ref[0], place_ref[1], place_ref[2]

    def block(d):
        start = lax.rem(piece + d, n) * tile
        return green_ref[pl.ds(pl.multiple_of(start, tile), tile), :]

    planes, each = known_ref.shape[0], known_ref.shape[1]
    source = jnp.zeros((1, half), F32)
    for r in range(planes):
        for k in range(each):
            source = source + basis_ref[core, (plane ^ r) * each + k] * known_ref[r, k : k + 1, :]
    source = jnp.concatenate((source, source), axis=1)
    scaled = (block(0).astype(F32) * source).astype(BF16)
    turned = jnp.concatenate((scaled[:, half:], -scaled[:, :half]), axis=1)
    both = jnp.concatenate((scaled, turned), axis=0)
    pair = across(both, block(0))
    row = lax.broadcasted_iota(jnp.int32, (tile, tile), 0)
    col = lax.broadcasted_iota(jnp.int32, (tile, tile), 1)
    out_ref[:, :tile] = jnp.where(row >= col, pair[:tile], pair[tile:]).astype(out_ref.dtype)
    for d in range(1, n // 2):
        pair = across(both, block(d)).astype(out_ref.dtype)
        out_ref[:, (2 * d - 1) * tile : 2 * d * tile] = pair[:tile]
        out_ref[:, 2 * d * tile : (2 * d + 1) * tile] = pair[tile:]
    last = across(jnp.where(piece < n // 2, scaled, turned), block(n // 2))
    out_ref[:, (n - 1) * tile :] = last.astype(out_ref.dtype)


def sens_kernel(n, step, piece_ref, resid_ref, green_ref, out_ref):
    stations, width = green_ref.shape
    tile, half = stations // n, width // 2
    piece = piece_ref[0]
    starts = [pl.multiple_of(lax.rem(piece + d, n) * tile, tile) for d in range(n // 2 + 1)]
    row = lax.broadcasted_iota(jnp.int32, (tile, tile), 0)
    col = lax.broadcasted_iota(jnp.int32, (tile, tile), 1)
    diag = resid_ref[:, :tile].astype(F32)
    lower = jnp.where(row > col, diag, jnp.where(row == col, 0.5 * diag, 0.0)).astype(BF16)
    upper = jnp.where(row < col, diag, 0.0).astype(BF16)
    last = resid_ref[:, (n - 1) * tile :]
    real = piece < n // 2
    for at in range(0, half, step):

        def fields(d):
            rows = pl.ds(starts[d], tile)
            return green_ref[rows, at : at + step], green_ref[rows, half + at : half + at + step]

        re_here, im_here = fields(0)
        pu, pv = along(lower, re_here), along(lower, im_here)
        qu, qv = along(upper, re_here), along(upper, im_here)
        for d in range(1, n // 2):
            re, im = fields(d)
            p = resid_ref[:, (2 * d - 1) * tile : 2 * d * tile]
            q = resid_ref[:, 2 * d * tile : (2 * d + 1) * tile]
            pu, pv = pu + along(p, re), pv + along(p, im)
            qu, qv = qu + along(q, re), qv + along(q, im)
        re, im = fields(n // 2)
        hu, hv = along(last, re), along(last, im)
        yre = pu - qv + jnp.where(real, hu, -hv)
        yim = pv + qu + jnp.where(real, hv, hu)
        share = re_here.astype(F32) * yre + im_here.astype(F32) * yim
        out_ref[:, at : at + step] = 2.0 * jnp.sum(share, axis=0, keepdims=True)


def hess_kernel(planes, place_ref, basis_ref, sens_ref, other_ref, out_ref):
    core, plane = place_ref[0], place_ref[1]
    each = out_ref.shape[0] // planes
    mine, other = sens_ref[:, : out_ref.shape[1]], other_ref[...]
    for r in range(planes):
        for k in range(each):
            b, i = (plane ^ r) * each + k, r * each + k
            out_ref[i : i + 1, :] = basis_ref[core, b] * mine + basis_ref[1 - core, b] * other


SMEM = pl.BlockSpec(memory_space=pltpu.SMEM)
VMEM = pl.BlockSpec(memory_space=pltpu.VMEM)
HBM = pl.BlockSpec(memory_space=pltpu.HBM)


def call(kernel, shape, dtype, specs, flops, moved, grant, *args, scratch=()):
    return pl.pallas_call(
        kernel,
        out_shape=jax.ShapeDtypeStruct(shape, dtype),
        in_specs=specs,
        out_specs=VMEM,
        scratch_shapes=scratch,
        compiler_params=pltpu.CompilerParams(vmem_limit_bytes=grant * MIB),
        cost_estimate=pl.CostEstimate(flops=flops, bytes_accessed=moved, transcendentals=0),
    )(*args)


def on_device(n_freq, n_cell, green, coeffs, basis, amplitude, block_mask):
    n = n_cell // 2
    bits, z_bits = n.bit_length() - 1, n_freq.bit_length() - 1
    stations, cells = green.shape[2], green.shape[3]
    tile, width, each = stations // n, 4 * cells, coeffs.shape[0]
    here = lax.axis_index("cell").astype(jnp.int32)
    plane = lax.axis_index("freq").astype(jnp.int32)
    core, chip = here % 2, here // 2
    flops = 2 * tile * stations * width * 5 // 4
    moved = 2 * stations * width + 2 * tile * stations

    def dims(which):
        return [(which + j) % bits for j in range(bits)]

    swap_core = [(i, i ^ 1) for i in range(n_cell)]

    def swap_chip(value, j):
        pairs = [(i, i ^ (2 << dims(i % 2)[j])) for i in range(n_cell)]
        return lax.ppermute(value, "cell", pairs)

    def swap_plane(value, j):
        return lax.ppermute(value, "freq", [(i, i ^ (1 << j)) for i in range(n_freq)])

    def piece_of(q):
        flips = [sum(((q >> j) & 1) << dims(which)[j] for j in range(bits)) for which in (0, 1)]
        return chip ^ jnp.where(core == 0, flips[0], flips[1])

    beside = lax.ppermute(coeffs, "cell", swap_core)
    core_only = core.reshape(1)
    two = [pltpu.SemaphoreType.DMA((2,))]
    theirs = call(
        take_kernel, (2, stations, cells), BF16, [SMEM, HBM], 0,
        8 * stations * cells, 50, core_only, green, scratch=two,
    )
    theirs = lax.ppermute(theirs, "cell", swap_core)
    known = jnp.concatenate((coeffs, beside), axis=1)[None]
    for j in range(z_bits):
        near = swap_plane(known, j)
        known = jnp.concatenate((known, near), axis=0)

    field = call(
        field_kernel, (stations, width), BF16, [SMEM, HBM, HBM], 0,
        4 * stations * width, 45, core_only, green, theirs, scratch=[pltpu.SemaphoreType.DMA((4,))],
    )

    def corr_piece(q):
        return call(
            functools.partial(corr_kernel, n), (tile, stations), F32 if q % 2 == 0 else BF16,
            [SMEM, SMEM, VMEM, VMEM], flops, moved, 24,
            jnp.stack((core, plane, piece_of(q))), basis, known, field,
        )

    held = {}
    for q in sorted(range(n), key=lambda q: (q % 2 == 0, -q)):
        held[q] = corr_piece(q)
    weight = call(
        functools.partial(weight_kernel, n), (tile, stations), F32, [SMEM, VMEM, VMEM],
        0, 4 * tile * stations, 8, jnp.stack((core, piece_of(0))), amplitude, block_mask,
    )
    for j in range(bits):
        for q in sorted((q for q in held if (q >> j) & 1), reverse=True):
            got = swap_chip(held.pop(q).astype(BF16), j)
            rest = q ^ (1 << j)
            held[rest] = held[rest] + got.astype(F32)
    resid = {0: (held[0] * weight).astype(BF16)}

    def sens_piece(q):
        return call(
            functools.partial(sens_kernel, n, min(512, width // 2)), (1, width // 2), F32,
            [SMEM, VMEM, VMEM], flops, moved, 24, piece_of(q).reshape(1), resid[q], field,
        )

    sens = {}
    for j in reversed(range(bits)):
        for q in sorted(resid):
            if q == 0 and 0 in sens:
                sent, sens[0] = lax.optimization_barrier((resid[0], sens[0]))
            else:
                sent = resid[q]
            resid[q | (1 << j)] = swap_chip(sent, j)
            if 0 not in sens:
                sens[0] = sens_piece(0)
    for q in sorted(resid):
        if q not in sens:
            sens[q] = sens_piece(q)
    total = sum(sens.values())

    other = lax.ppermute(total[:, cells:], "cell", swap_core)
    partial = call(
        functools.partial(hess_kernel, n_freq), (n_freq * each, cells), F32,
        [SMEM, SMEM, VMEM, VMEM], 0, 4 * n_freq * each * cells, 4,
        jnp.stack((core, plane)), basis, total, other,
    )
    for j in reversed(range(z_bits)):
        middle = partial.shape[0] // 2
        partial = partial[:middle] + swap_plane(partial[middle:], j)
    return partial


def solution(mesh):
    placed = (
        P(None, "freq", None, "cell"),
        P("freq", "cell"),
        P("freq", None),
        P("freq", None),
        P(),
    )
    n_freq, n_cell = mesh.shape["freq"], mesh.shape["cell"]

    def body(*args):
        return on_device(n_freq, n_cell, *args)

    return jax.shard_map(
        body, mesh=mesh, in_specs=placed, out_specs=P("freq", "cell"), check_vma=False
    )
```

```python
import functools

import jax
import jax.numpy as jnp
from jax import lax
from jax.experimental import pallas as pl
from jax.experimental.pallas import tpu as pltpu
from jax.sharding import PartitionSpec as P


F32 = jnp.float32
BF16 = jnp.bfloat16
MIB = 1 << 20


def across(left, right):
    return lax.dot_general(left, right, (((1,), (1,)), ((), ())), preferred_element_type=F32)


def along(left, right):
    return jnp.dot(left, right, preferred_element_type=F32)


def copy_all(sems, pairs):
    copies = [pltpu.make_async_copy(src, dst, sems.at[i]) for i, (src, dst) in enumerate(pairs)]
    for copy in copies:
        copy.start()
    for copy in copies:
        copy.wait()


def take_kernel(core_ref, green_ref, out_ref, sems):
    other = 1 - core_ref[0]
    copy_all(sems, [(green_ref.at[p, other], out_ref.at[p]) for p in (0, 1)])


def mine_kernel(core_ref, green_ref, out_ref, sems):
    core, cells = core_ref[0], green_ref.shape[3]
    spots = [out_ref.at[:, pl.ds(2 * p * cells, cells)] for p in (0, 1)]
    copy_all(sems, [(green_ref.at[p, core], spots[p]) for p in (0, 1)])


def theirs_kernel(theirs_ref, field_ref, out_ref, sems):
    del field_ref
    cells = theirs_ref.shape[2]
    spots = [out_ref.at[:, pl.ds((2 * p + 1) * cells, cells)] for p in (0, 1)]
    copy_all(sems, [(theirs_ref.at[p], spots[p]) for p in (0, 1)])


def weight_kernel(n, place_ref, amp_ref, mask_ref, *out_refs):
    core, piece = place_ref[0], place_ref[1]
    tile = out_refs[0].shape[0]
    blocks = mask_ref.shape[0]
    size = n * tile // blocks

    def amp(start):
        both = amp_ref[:, pl.ds(pl.multiple_of(start, tile), tile)]
        return jnp.where(core == 0, both[0:1], both[1:2])

    here = piece * tile
    row = lax.broadcasted_iota(jnp.int32, (tile, tile), 0)
    col = lax.broadcasted_iota(jnp.int32, (tile, tile), 1)
    down = jnp.sum(jnp.where(row == col, amp(here), 0.0), axis=1, keepdims=True)
    mask = mask_ref[...].astype(BF16)
    low = lax.broadcasted_iota(jnp.int32, (tile, blocks), 1) * size
    at = here + lax.broadcasted_iota(jnp.int32, (tile, blocks), 0)
    pick = ((at >= low) & (at < low + size)).astype(BF16)
    rows = (0.5 * (along(pick, mask) + across(pick, mask))).astype(BF16)
    low = lax.broadcasted_iota(jnp.int32, (blocks, tile), 0) * size
    for d in range(n // 2 + 1):
        start = lax.rem(piece + d, n) * tile
        at = start + lax.broadcasted_iota(jnp.int32, (blocks, tile), 1)
        pick = ((at >= low) & (at < low + size)).astype(BF16)
        weight = down * amp(start) * along(rows, pick)
        for i in [0] if d == 0 else [n - 1] if d == n // 2 else [2 * d - 1, 2 * d]:
            u, at_block = divmod(i, n // 2)
            out_refs[u][:, at_block * tile : (at_block + 1) * tile] = weight


def corr_kernel(n, halves, place_ref, basis_ref, known_ref, green_ref, *out_refs):
    stations, width = green_ref.shape
    tile, half = stations // n, width // 2
    core, plane, piece = place_ref[0], place_ref[1], place_ref[2]

    def block(d):
        start = lax.rem(piece + d, n) * tile
        return green_ref[pl.ds(pl.multiple_of(start, tile), tile), :]

    def put(i, value):
        u, at = divmod(i, n // 2)
        out_ref = out_refs[halves.index(u)]
        out_ref[:, at * tile : (at + 1) * tile] = value.astype(out_ref.dtype)

    source = jnp.sum(basis_column(core, plane, basis_ref, known_ref.shape[0]) * known_ref[...], 0, keepdims=True)
    source = jnp.concatenate((source, source), axis=1)
    scaled = (block(0).astype(F32) * source).astype(BF16)
    turned = jnp.concatenate((scaled[:, half:], -scaled[:, :half]), axis=1)
    both = jnp.concatenate((scaled, turned), axis=0)
    wanted = [i for u in halves for i in range(u * (n // 2), (u + 1) * (n // 2))]
    if 0 in wanted:
        pair = across(both, block(0))
        row = lax.broadcasted_iota(jnp.int32, (tile, tile), 0)
        col = lax.broadcasted_iota(jnp.int32, (tile, tile), 1)
        put(0, jnp.where(row >= col, pair[:tile], pair[tile:]))
    for d in range(1, n // 2):
        if 2 * d - 1 in wanted and 2 * d in wanted:
            pair = across(both, block(d))
            put(2 * d - 1, pair[:tile])
            put(2 * d, pair[tile:])
        elif 2 * d - 1 in wanted:
            put(2 * d - 1, across(scaled, block(d)))
        elif 2 * d in wanted:
            put(2 * d, across(turned, block(d)))
    if n - 1 in wanted:
        put(n - 1, across(jnp.where(piece < n // 2, scaled, turned), block(n // 2)))


def basis_column(core, plane, basis_ref, count):
    each = count // PLANES[0]
    at = lax.broadcasted_iota(jnp.int32, (count, 1), 0)
    column = jnp.zeros((count, 1), F32)
    for i in range(count):
        column = jnp.where(at == i, basis_ref[core, (plane ^ (i // each)) * each + i % each], column)
    return column


PLANES = [0]


def sens_sum(n, u, step, piece, resid_ref, green_ref, emit):
    stations, width = green_ref.shape
    tile, half = stations // n, width // 2
    starts = [pl.multiple_of(lax.rem(piece + d, n) * tile, tile) for d in range(n // 2 + 1)]
    real = piece < n // 2
    terms = []
    for i in range(u * (n // 2), (u + 1) * (n // 2)):
        at = (i - u * (n // 2)) * tile
        value = resid_ref[:, at : at + tile]
        if i == 0:
            row = lax.broadcasted_iota(jnp.int32, (tile, tile), 0)
            col = lax.broadcasted_iota(jnp.int32, (tile, tile), 1)
            diag = value.astype(F32)
            low = jnp.where(row > col, diag, jnp.where(row == col, 0.5 * diag, 0.0))
            terms.append(("re", 0, low.astype(BF16)))
            terms.append(("im", 0, jnp.where(row < col, diag, 0.0).astype(BF16)))
        elif i == n - 1:
            terms.append(("either", n // 2, value))
        else:
            terms.append(("re" if i % 2 else "im", (i + 1) // 2, value))
    for at in range(0, half, step):

        def fields(d):
            rows = pl.ds(starts[d], tile)
            return green_ref[rows, at : at + step], green_ref[rows, half + at : half + at + step]

        yre, yim = jnp.zeros((tile, step), F32), jnp.zeros((tile, step), F32)
        for kind, d, value in terms:
            re, im = fields(d)
            tu, tv = along(value, re), along(value, im)
            if kind == "re":
                yre, yim = yre + tu, yim + tv
            elif kind == "im":
                yre, yim = yre - tv, yim + tu
            else:
                yre, yim = yre + jnp.where(real, tu, -tv), yim + jnp.where(real, tv, tu)
        re, im = fields(0)
        share = re.astype(F32) * yre + im.astype(F32) * yim
        emit(at, 2.0 * jnp.sum(share, axis=0, keepdims=True))


def sens_kernel(n, u, step, piece_ref, resid_ref, green_ref, out_ref):
    def emit(at, value):
        out_ref[:, at : at + step] = value

    sens_sum(n, u, step, piece_ref[0], resid_ref, green_ref, emit)


def last_kernel(n, u, step, place_ref, basis_ref, before_ref, resid_ref, green_ref, *out_refs):
    core, plane = place_ref[0], place_ref[1]
    rows = out_refs[0].shape[0]
    column = basis_column(core, plane, basis_ref, rows * len(out_refs))

    def emit(at, value):
        product = column * (before_ref[:, at : at + step] + value)
        for k, out_ref in enumerate(out_refs):
            out_ref[:, at : at + step] = product[k * rows : (k + 1) * rows]

    sens_sum(n, u, step, place_ref[2], resid_ref, green_ref, emit)


SMEM = pl.BlockSpec(memory_space=pltpu.SMEM)
VMEM = pl.BlockSpec(memory_space=pltpu.VMEM)
HBM = pl.BlockSpec(memory_space=pltpu.HBM)


def call(kernel, shapes, dtype, specs, flops, moved, grant, *args, scratch=(), alias={}):
    out_shape = [jax.ShapeDtypeStruct(shape, dtype) for shape in shapes]
    out = pl.pallas_call(
        kernel,
        out_shape=out_shape,
        in_specs=specs,
        out_specs=[VMEM] * len(shapes),
        scratch_shapes=scratch,
        input_output_aliases=alias,
        compiler_params=pltpu.CompilerParams(vmem_limit_bytes=grant * MIB),
        cost_estimate=pl.CostEstimate(flops=flops, bytes_accessed=moved, transcendentals=0),
    )(*args)
    return out if len(out) > 1 else out[0]


def on_device(n_freq, n_cell, green, coeffs, basis, amplitude, block_mask):
    n = n_cell // 2
    bits, z_bits = n.bit_length() - 1, n_freq.bit_length() - 1
    stations, cells = green.shape[2], green.shape[3]
    tile, width, each = stations // n, 4 * cells, coeffs.shape[0]
    PLANES[0] = n_freq
    here = lax.axis_index("cell").astype(jnp.int32)
    plane = lax.axis_index("freq").astype(jnp.int32)
    core, chip = here % 2, here // 2
    flops = tile * stations * width * 5 // 4
    moved = 2 * stations * width + 2 * tile * stations

    def dims(which):
        return [(which + j) % bits for j in range(bits)]

    swap_core = [(i, i ^ 1) for i in range(n_cell)]

    def swap_chip(value, j):
        pairs = [(i, i ^ (2 << dims(i % 2)[j])) for i in range(n_cell)]
        return lax.ppermute(value, "cell", pairs)

    def swap_plane(value, j):
        return lax.ppermute(value, "freq", [(i, i ^ (1 << j)) for i in range(n_freq)])

    def piece_of(q):
        flips = [sum(((q >> j) & 1) << dims(which)[j] for j in range(bits)) for which in (0, 1)]
        return chip ^ jnp.where(core == 0, flips[0], flips[1])

    beside = lax.ppermute(coeffs, "cell", swap_core)
    core_only = core.reshape(1)
    placed_green = pltpu.with_memory_space_constraint(green, pltpu.HBM)
    two = [pltpu.SemaphoreType.DMA((2,))]
    theirs = call(
        take_kernel, [(2, stations, cells)], BF16, [SMEM, HBM], 0,
        8 * stations * cells, 16, core_only, placed_green, scratch=two,
    )
    theirs = lax.ppermute(theirs, "cell", swap_core)
    theirs = pltpu.with_memory_space_constraint(theirs, pltpu.HBM)
    known = jnp.concatenate((coeffs, beside), axis=1)
    for j in range(z_bits):
        near = swap_plane(known, j)
        known = jnp.concatenate((known, near), axis=0)

    field = call(
        mine_kernel, [(stations, width)], BF16, [SMEM, HBM], 0,
        2 * stations * width, 16, core_only, placed_green, scratch=two,
    )
    field = call(
        theirs_kernel, [(stations, width)], BF16, [HBM, VMEM], 0,
        2 * stations * width, 45, theirs, field, scratch=two, alias={1: 0},
    )

    def corr_piece(q, halves, dtype):
        out = call(
            functools.partial(corr_kernel, n, halves), [(tile, stations // 2)] * len(halves), dtype,
            [SMEM, SMEM, VMEM, VMEM], flops * len(halves), moved, 24,
            jnp.stack((core, plane, piece_of(q))), basis, known, field,
        )
        return out if len(halves) > 1 else [out]

    held = {}
    for q in sorted(range(n), key=lambda q: (q % 2 == 0, -q)):
        if q % 2:
            for u in (0, 1):
                held[q, u] = corr_piece(q, (u,), BF16)[0]
        else:
            held[q, 0], held[q, 1] = corr_piece(q, (0, 1), F32)
    weight = call(
        functools.partial(weight_kernel, n), [(tile, stations // 2)] * 2, F32, [SMEM, VMEM, VMEM],
        0, 4 * tile * stations, 8, jnp.stack((core, piece_of(0))), amplitude, block_mask,
    )
    for j in range(bits):
        for q in sorted((q for q in range(n) if q % (1 << j) == 0 and (q >> j) & 1), reverse=True):
            for u in (0, 1):
                got = swap_chip(held[q, u].astype(BF16), j)
                held[q ^ (1 << j), u] = held[q ^ (1 << j), u] + got.astype(F32)
    resid = {(0, u): (held[0, u] * weight[u]).astype(BF16) for u in (0, 1)}

    order = [0]
    for j in reversed(range(bits)):
        for q in list(order):
            order.append(q | (1 << j))
            for u in (0, 1):
                resid[order[-1], u] = swap_chip(resid[q, u], j)
    step = min(512, width // 2)
    sens = 0.0
    for q in order:
        for u in (0, 1):
            if (q, u) == (order[-1], 1):
                continue
            sens = sens + call(
                functools.partial(sens_kernel, n, u, step), [(1, width // 2)], F32,
                [SMEM, VMEM, VMEM], flops, moved, 24, piece_of(q).reshape(1), resid[q, u], field,
            )
    rows = n_freq * each // 2
    low, high = call(
        functools.partial(last_kernel, n, 1, step), [(rows, width // 2)] * 2, F32,
        [SMEM, SMEM, VMEM, VMEM, VMEM], flops, moved, 24,
        jnp.stack((core, plane, piece_of(order[-1]))), basis, sens, resid[order[-1], 1], field,
    )

    for j in reversed(range(z_bits)):
        kept = low + swap_plane(high, j)
        low, high = kept[: kept.shape[0] // 2], kept[kept.shape[0] // 2 :]
    return kept[:, :cells] + lax.ppermute(kept[:, cells:], "cell", swap_core)


def solution(mesh):
    placed = (
        P(None, "freq", None, "cell"),
        P("freq", "cell"),
        P("freq", None),
        P("freq", None),
        P(),
    )
    n_freq, n_cell = mesh.shape["freq"], mesh.shape["cell"]

    def body(*args):
        return on_device(n_freq, n_cell, *args)

    return jax.shard_map(
        body, mesh=mesh, in_specs=placed, out_specs=P("freq", "cell"), check_vma=False
    )
```

```python
import functools

import jax
import jax.numpy as jnp
from jax import lax
from jax.experimental import pallas as pl
from jax.experimental.pallas import tpu as pltpu
from jax.sharding import PartitionSpec as P


F32 = jnp.float32
BF16 = jnp.bfloat16
MIB = 1 << 20


def across(left, right):
    return lax.dot_general(left, right, (((1,), (1,)), ((), ())), preferred_element_type=F32)


def along(left, right):
    return jnp.dot(left, right, preferred_element_type=F32)


def start_all(sems, pairs):
    copies = [pltpu.make_async_copy(src, dst, sems.at[i]) for i, (src, dst) in enumerate(pairs)]
    for copy in copies:
        copy.start()
    return copies


def weight_kernel(n, core_ref, piece_ref, amp_ref, mask_ref, *weight_refs):
    core, piece = core_ref[0], piece_ref[0]
    tile = weight_refs[0].shape[0]
    blocks = mask_ref.shape[0]
    size = n * tile // blocks

    def amp(start):
        both = amp_ref[:, pl.ds(pl.multiple_of(start, tile), tile)]
        return jnp.where(core == 0, both[0:1], both[1:2])

    here = piece * tile
    row = lax.broadcasted_iota(jnp.int32, (tile, tile), 0)
    col = lax.broadcasted_iota(jnp.int32, (tile, tile), 1)
    down = jnp.sum(jnp.where(row == col, amp(here), 0.0), axis=1, keepdims=True)
    mask = mask_ref[...].astype(BF16)
    low = lax.broadcasted_iota(jnp.int32, (tile, blocks), 1) * size
    at = here + lax.broadcasted_iota(jnp.int32, (tile, blocks), 0)
    pick = ((at >= low) & (at < low + size)).astype(BF16)
    rows = (0.5 * (along(pick, mask) + across(pick, mask))).astype(BF16)
    low = lax.broadcasted_iota(jnp.int32, (blocks, tile), 0) * size
    for d in range(n // 2 + 1):
        start = lax.rem(piece + d, n) * tile
        at = start + lax.broadcasted_iota(jnp.int32, (blocks, tile), 1)
        pick = ((at >= low) & (at < low + size)).astype(BF16)
        weight = down * amp(start) * along(rows, pick)
        for i in [0] if d == 0 else [n - 1] if d == n // 2 else [2 * d - 1, 2 * d]:
            u, at_block = divmod(i, n // 2)
            weight_refs[u][:, at_block * tile : (at_block + 1) * tile] = weight


def take_kernel(core_ref, green_ref, *rest):
    out_ref, sems = rest[-2:]
    other = 1 - core_ref[0]
    for copy in start_all(sems, [(green_ref.at[p, other], out_ref.at[p]) for p in (0, 1)]):
        copy.wait()


def mine_kernel(core_ref, green_ref, out_ref, sems):
    core, cells = core_ref[0], green_ref.shape[3]
    spots = [out_ref.at[:, pl.ds(2 * p * cells, cells)] for p in (0, 1)]
    for copy in start_all(sems, [(green_ref.at[p, core], spots[p]) for p in (0, 1)]):
        copy.wait()


def theirs_kernel(planes, core_ref, plane_ref, basis_ref, theirs_ref, field_ref, out_ref, column_ref, sems):
    del field_ref
    core, plane, cells = core_ref[0], plane_ref[0], theirs_ref.shape[2]
    spots = [out_ref.at[:, pl.ds((2 * p + 1) * cells, cells)] for p in (0, 1)]
    copies = start_all(sems, [(theirs_ref.at[p], spots[p]) for p in (0, 1)])
    each = column_ref.shape[0] // planes
    at = lax.broadcasted_iota(jnp.int32, column_ref.shape, 0)
    column = jnp.zeros(column_ref.shape, F32)
    for i in range(column_ref.shape[0]):
        column = jnp.where(at == i, basis_ref[core, (plane ^ (i // each)) * each + i % each], column)
    column_ref[...] = column
    for copy in copies:
        copy.wait()


def corr_kernel(n, parts, piece_ref, column_ref, known_ref, green_ref, *out_refs):
    stations, width = green_ref.shape
    tile, half = stations // n, width // 2
    piece = piece_ref[0]

    def block(d):
        start = lax.rem(piece + d, n) * tile
        return green_ref[pl.ds(pl.multiple_of(start, tile), tile), :]

    def put(i, value):
        for part, out_ref in zip(parts, out_refs):
            if i in part:
                at = (i - part[0]) * tile
                out_ref[:, at : at + tile] = value.astype(out_ref.dtype)

    source = jnp.sum(column_ref[:, 0:1] * known_ref[...], axis=0, keepdims=True)
    source = jnp.concatenate((source, source), axis=1)
    scaled = (block(0).astype(F32) * source).astype(BF16)
    turned = jnp.concatenate((scaled[:, half:], -scaled[:, :half]), axis=1)
    both = jnp.concatenate((scaled, turned), axis=0)
    wanted = [i for part in parts for i in part]
    if 0 in wanted:
        pair = across(both, block(0))
        row = lax.broadcasted_iota(jnp.int32, (tile, tile), 0)
        col = lax.broadcasted_iota(jnp.int32, (tile, tile), 1)
        put(0, jnp.where(row >= col, pair[:tile], pair[tile:]))
    for d in range(1, n // 2):
        if 2 * d - 1 in wanted and 2 * d in wanted:
            pair = across(both, block(d))
            put(2 * d - 1, pair[:tile])
            put(2 * d, pair[tile:])
        elif 2 * d - 1 in wanted:
            put(2 * d - 1, across(scaled, block(d)))
        elif 2 * d in wanted:
            put(2 * d, across(turned, block(d)))
    if n - 1 in wanted:
        put(n - 1, across(jnp.where(piece < n // 2, scaled, turned), block(n // 2)))


def sens_sum(n, part, step, piece, resid_ref, green_ref, emit):
    stations, width = green_ref.shape
    tile, half = stations // n, width // 2
    starts = [pl.multiple_of(lax.rem(piece + d, n) * tile, tile) for d in range(n // 2 + 1)]
    real = piece < n // 2
    terms = []
    for i in part:
        at = (i - part[0]) * tile
        value = resid_ref[:, at : at + tile]
        if i == 0:
            row = lax.broadcasted_iota(jnp.int32, (tile, tile), 0)
            col = lax.broadcasted_iota(jnp.int32, (tile, tile), 1)
            diag = value.astype(F32)
            low = jnp.where(row > col, diag, jnp.where(row == col, 0.5 * diag, 0.0))
            terms.append(("re", 0, low.astype(BF16)))
            terms.append(("im", 0, jnp.where(row < col, diag, 0.0).astype(BF16)))
        elif i == n - 1:
            terms.append(("either", n // 2, value))
        else:
            terms.append(("re" if i % 2 else "im", (i + 1) // 2, value))
    for at in range(0, half, step):

        def fields(d):
            rows = pl.ds(starts[d], tile)
            return green_ref[rows, at : at + step], green_ref[rows, half + at : half + at + step]

        yre, yim = jnp.zeros((tile, step), F32), jnp.zeros((tile, step), F32)
        for kind, d, value in terms:
            re, im = fields(d)
            tu, tv = along(value, re), along(value, im)
            if kind == "re":
                yre, yim = yre + tu, yim + tv
            elif kind == "im":
                yre, yim = yre - tv, yim + tu
            else:
                yre, yim = yre + jnp.where(real, tu, -tv), yim + jnp.where(real, tv, tu)
        re, im = fields(0)
        share = re.astype(F32) * yre + im.astype(F32) * yim
        emit(at, 2.0 * jnp.sum(share, axis=0, keepdims=True))


def sens_kernel(n, part, step, piece_ref, resid_ref, green_ref, out_ref):
    def emit(at, value):
        out_ref[:, at : at + step] = value

    sens_sum(n, part, step, piece_ref[0], resid_ref, green_ref, emit)


def last_kernel(n, part, step, piece_ref, column_ref, before_ref, resid_ref, green_ref, *out_refs):
    rows = out_refs[0].shape[0]
    column = column_ref[:, 0:1]

    def emit(at, value):
        product = column * (before_ref[:, at : at + step] + value)
        for k, out_ref in enumerate(out_refs):
            out_ref[:, at : at + step] = product[k * rows : (k + 1) * rows]

    sens_sum(n, part, step, piece_ref[0], resid_ref, green_ref, emit)


def first_sent(n):
    return n - 1, 0


SMEM = pl.BlockSpec(memory_space=pltpu.SMEM)
VMEM = pl.BlockSpec(memory_space=pltpu.VMEM)
HBM = pl.BlockSpec(memory_space=pltpu.HBM)


def call(kernel, shapes, specs, flops, moved, *args, scratch=(), alias={}, grant=24):
    out_shape = [jax.ShapeDtypeStruct(shape, dtype) for shape, dtype in shapes]
    out = pl.pallas_call(
        kernel,
        out_shape=out_shape,
        in_specs=specs,
        out_specs=[VMEM] * len(shapes),
        scratch_shapes=scratch,
        input_output_aliases=alias,
        compiler_params=pltpu.CompilerParams(vmem_limit_bytes=grant * MIB),
        cost_estimate=pl.CostEstimate(flops=flops, bytes_accessed=moved, transcendentals=0),
    )(*args)
    return out if len(out) > 1 else out[0]


def on_device(n_freq, n_cell, green, coeffs, basis, amplitude, block_mask):
    n = n_cell // 2
    bits, z_bits = n.bit_length() - 1, n_freq.bit_length() - 1
    stations, cells = green.shape[2], green.shape[3]
    tile, width, each = stations // n, 4 * cells, coeffs.shape[0]
    here = lax.axis_index("cell").astype(jnp.int32)
    plane = lax.axis_index("freq").astype(jnp.int32)
    core, chip = here % 2, here // 2
    flops = 2 * tile * tile * width
    moved = 2 * stations * width + 2 * tile * stations
    halves = [tuple(range(u * n // 2, (u + 1) * n // 2)) for u in (0, 1)]

    def dims(which):
        return [(which + j) % bits for j in range(bits)]

    swap_core = [(i, i ^ 1) for i in range(n_cell)]

    def swap_chip(value, j):
        pairs = [(i, i ^ (2 << dims(i % 2)[j])) for i in range(n_cell)]
        return lax.ppermute(value, "cell", pairs)

    def swap_plane(value, j):
        return lax.ppermute(value, "freq", [(i, i ^ (1 << j)) for i in range(n_freq)])

    def piece_of(q):
        flips = [sum(((q >> j) & 1) << dims(which)[j] for j in range(bits)) for which in (0, 1)]
        return chip ^ jnp.where(core == 0, flips[0], flips[1])

    cores, planes = core.reshape(1), plane.reshape(1)
    pieces = [piece_of(q).reshape(1) for q in range(n)]
    green = pltpu.with_memory_space_constraint(green, pltpu.HBM)
    two = [pltpu.SemaphoreType.DMA((2,))]
    theirs = call(
        take_kernel, [((2, stations, cells), BF16)], [SMEM, HBM] + [SMEM] * (n + 1), 0,
        8 * stations * cells, cores, green, planes, *pieces, scratch=two,
    )
    theirs = lax.ppermute(theirs, "cell", swap_core)
    known = coeffs
    for j in range(z_bits):
        near = swap_plane(known, j)
        known = jnp.concatenate((known, near), axis=0)
    beside = lax.ppermute(known, "cell", swap_core)
    known = jnp.concatenate((known, beside), axis=1)

    field = call(
        mine_kernel, [((stations, width), BF16)], [SMEM, HBM], 0,
        2 * stations * width, cores, green, scratch=two,
    )
    field, column = call(
        functools.partial(theirs_kernel, n_freq),
        [((stations, width), BF16), ((n_freq * each, 128), F32)], [SMEM, SMEM, SMEM, VMEM, VMEM], 0,
        2 * stations * width, cores, planes, basis, theirs, field, scratch=two, alias={4: 0},
    )

    def corr_parts(q, parts, dtype):
        shapes = [((tile, len(part) * tile), dtype) for part in parts]
        out = call(
            functools.partial(corr_kernel, n, parts), shapes, [SMEM, VMEM, VMEM, VMEM],
            flops * sum(len(part) for part in parts), moved, pieces[q], column, known, field,
        )
        return out if len(parts) > 1 else [out]

    held = {}
    for q in sorted(range(n), key=lambda q: (q % 2 == 0, -q)):
        if q % 2 == 0:
            held[q, 0], held[q, 1] = corr_parts(q, halves, F32)
            continue
        for u in (0, 1):
            if (q, u) == first_sent(n):
                middle = n // 4
                held[q, "b"] = corr_parts(q, [halves[u][middle:]], BF16)[0]
                held[q, "a"] = corr_parts(q, [halves[u][:middle]], BF16)[0]
            else:
                held[q, u] = corr_parts(q, [halves[u]], BF16)[0]
    weight = call(
        functools.partial(weight_kernel, n), [((tile, stations // 2), F32)] * 2,
        [SMEM, SMEM, VMEM, VMEM], 0, 4 * tile * stations, cores, pieces[0], amplitude, block_mask,
    )
    for j in range(bits):
        for q in sorted((q for q in range(n) if q % (1 << j) == 0 and (q >> j) & 1), reverse=True):
            for u in (0, 1):
                if (q, u) == first_sent(n):
                    late, early = (swap_chip(held[q, k], j) for k in "ab")
                    got = jnp.concatenate((late, early), axis=1)
                else:
                    got = swap_chip(held[q, u].astype(BF16), j)
                held[q ^ (1 << j), u] = held[q ^ (1 << j), u] + got.astype(F32)
    resid = {(0, u): (held[0, u] * weight[u]).astype(BF16) for u in (0, 1)}

    order, parts = [0], {"0": halves[0], "1": halves[1], "c": halves[1][: n // 4], "d": halves[1][n // 4 :]}
    for j in reversed(range(bits)):
        for q in list(order):
            order.append(q | (1 << j))
            for u in (0, 1):
                if (order[-1], u) == (n - 1, 1):
                    cut = n // 4 * tile
                    resid[n - 1, "c"] = swap_chip(resid[q, u][:, :cut], j)
                    resid[n - 1, "d"] = swap_chip(resid[q, u][:, cut:], j)
                else:
                    resid[order[-1], u] = swap_chip(resid[q, u], j)
    step = min(512, width // 2)
    sens = 0.0
    for (q, u), value in resid.items():
        if (q, u) == (n - 1, "d"):
            continue
        part = parts[str(u)]
        sens = sens + call(
            functools.partial(sens_kernel, n, part, step), [((1, width // 2), F32)],
            [SMEM, VMEM, VMEM], flops * len(part), moved, pieces[q], value, field,
        )
    half_rows = ((n_freq * each // 2, width // 2), F32)
    low, high = call(
        functools.partial(last_kernel, n, parts["d"], step), [half_rows] * 2,
        [SMEM, VMEM, VMEM, VMEM, VMEM], flops * (n // 4), moved,
        pieces[n - 1], column, sens, resid[n - 1, "d"], field,
    )

    for j in reversed(range(z_bits)):
        kept = low + swap_plane(high, j)
        low, high = kept[: kept.shape[0] // 2], kept[kept.shape[0] // 2 :]
    return kept[:, :cells] + lax.ppermute(kept[:, cells:], "cell", swap_core)


def solution(mesh):
    placed = (
        P(None, "freq", None, "cell"),
        P("freq", "cell"),
        P("freq", None),
        P("freq", None),
        P(),
    )
    n_freq, n_cell = mesh.shape["freq"], mesh.shape["cell"]

    def body(*args):
        return on_device(n_freq, n_cell, *args)

    return jax.shard_map(
        body, mesh=mesh, in_specs=placed, out_specs=P("freq", "cell"), check_vma=False
    )
```

```python
import functools

import jax
import jax.numpy as jnp
from jax import lax
from jax.experimental import pallas as pl
from jax.experimental.pallas import tpu as pltpu
from jax.sharding import PartitionSpec as P


F32 = jnp.float32
BF16 = jnp.bfloat16
MIB = 1 << 20


def across(left, right):
    return lax.dot_general(left, right, (((1,), (1,)), ((), ())), preferred_element_type=F32)


def along(left, right):
    return jnp.dot(left, right, preferred_element_type=F32)


def start_all(sems, pairs):
    copies = [pltpu.make_async_copy(src, dst, sems.at[i]) for i, (src, dst) in enumerate(pairs)]
    for copy in copies:
        copy.start()
    return copies


def weight_kernel(n, core_ref, piece_ref, amp_ref, mask_ref, *weight_refs):
    core, piece = core_ref[0], piece_ref[0]
    tile = weight_refs[0].shape[0]
    blocks = mask_ref.shape[0]
    size = n * tile // blocks

    def amp(start):
        both = amp_ref[:, pl.ds(pl.multiple_of(start, tile), tile)]
        return jnp.where(core == 0, both[0:1], both[1:2])

    here = piece * tile
    row = lax.broadcasted_iota(jnp.int32, (tile, tile), 0)
    col = lax.broadcasted_iota(jnp.int32, (tile, tile), 1)
    down = jnp.sum(jnp.where(row == col, amp(here), 0.0), axis=1, keepdims=True)
    mask = mask_ref[...].astype(BF16)
    low = lax.broadcasted_iota(jnp.int32, (tile, blocks), 1) * size
    at = here + lax.broadcasted_iota(jnp.int32, (tile, blocks), 0)
    pick = ((at >= low) & (at < low + size)).astype(BF16)
    rows = (0.5 * (along(pick, mask) + across(pick, mask))).astype(BF16)
    low = lax.broadcasted_iota(jnp.int32, (blocks, tile), 0) * size
    for d in range(n // 2 + 1):
        start = lax.rem(piece + d, n) * tile
        at = start + lax.broadcasted_iota(jnp.int32, (blocks, tile), 1)
        pick = ((at >= low) & (at < low + size)).astype(BF16)
        weight = down * amp(start) * along(rows, pick)
        for i in [0] if d == 0 else [n - 1] if d == n // 2 else [2 * d - 1, 2 * d]:
            u, at_block = divmod(i, n // 2)
            weight_refs[u][:, at_block * tile : (at_block + 1) * tile] = weight


def take_kernel(core_ref, green_ref, *rest):
    out_ref, sems = rest[-2:]
    other = 1 - core_ref[0]
    for copy in start_all(sems, [(green_ref.at[p, other], out_ref.at[p]) for p in (0, 1)]):
        copy.wait()


def mine_kernel(core_ref, green_ref, out_ref, sems):
    core, cells = core_ref[0], green_ref.shape[3]
    spots = [out_ref.at[:, pl.ds(2 * p * cells, cells)] for p in (0, 1)]
    for copy in start_all(sems, [(green_ref.at[p, core], spots[p]) for p in (0, 1)]):
        copy.wait()


def theirs_kernel(planes, core_ref, plane_ref, basis_ref, theirs_ref, field_ref, out_ref, column_ref, sems):
    del field_ref
    core, plane, cells = core_ref[0], plane_ref[0], theirs_ref.shape[2]
    spots = [out_ref.at[:, pl.ds((2 * p + 1) * cells, cells)] for p in (0, 1)]
    copies = start_all(sems, [(theirs_ref.at[p], spots[p]) for p in (0, 1)])
    each = column_ref.shape[0] // planes
    at = lax.broadcasted_iota(jnp.int32, column_ref.shape, 0)
    column = jnp.zeros(column_ref.shape, F32)
    for i in range(column_ref.shape[0]):
        column = jnp.where(at == i, basis_ref[core, (plane ^ (i // each)) * each + i % each], column)
    column_ref[...] = column
    for copy in copies:
        copy.wait()


def corr_kernel(n, parts, piece_ref, column_ref, known_ref, green_ref, *out_refs):
    stations, width = green_ref.shape
    tile, half = stations // n, width // 2
    piece = piece_ref[0]

    def block(d):
        start = lax.rem(piece + d, n) * tile
        return green_ref[pl.ds(pl.multiple_of(start, tile), tile), :]

    def put(i, value):
        for part, out_ref in zip(parts, out_refs):
            if i in part:
                at = (i - part[0]) * tile
                out_ref[:, at : at + tile] = value.astype(out_ref.dtype)

    source = jnp.sum(column_ref[:, 0:1] * known_ref[...], axis=0, keepdims=True)
    source = jnp.concatenate((source, source), axis=1)
    scaled = (block(0).astype(F32) * source).astype(BF16)
    turned = jnp.concatenate((scaled[:, half:], -scaled[:, :half]), axis=1)
    both = jnp.concatenate((scaled, turned), axis=0)
    wanted = [i for part in parts for i in part]
    if 0 in wanted:
        pair = across(both, block(0))
        row = lax.broadcasted_iota(jnp.int32, (tile, tile), 0)
        col = lax.broadcasted_iota(jnp.int32, (tile, tile), 1)
        put(0, jnp.where(row >= col, pair[:tile], pair[tile:]))
    for d in range(1, n // 2):
        if 2 * d - 1 in wanted and 2 * d in wanted:
            pair = across(both, block(d))
            put(2 * d - 1, pair[:tile])
            put(2 * d, pair[tile:])
        elif 2 * d - 1 in wanted:
            put(2 * d - 1, across(scaled, block(d)))
        elif 2 * d in wanted:
            put(2 * d, across(turned, block(d)))
    if n - 1 in wanted:
        put(n - 1, across(jnp.where(piece < n // 2, scaled, turned), block(n // 2)))


def sens_sum(n, part, step, piece, resid_ref, green_ref, emit):
    stations, width = green_ref.shape
    tile, half = stations // n, width // 2
    starts = [pl.multiple_of(lax.rem(piece + d, n) * tile, tile) for d in range(n // 2 + 1)]
    real = piece < n // 2
    terms = []
    for i in part:
        at = (i - part[0]) * tile
        value = resid_ref[:, at : at + tile]
        if i == 0:
            row = lax.broadcasted_iota(jnp.int32, (tile, tile), 0)
            col = lax.broadcasted_iota(jnp.int32, (tile, tile), 1)
            diag = value.astype(F32)
            low = jnp.where(row > col, diag, jnp.where(row == col, 0.5 * diag, 0.0))
            terms.append(("re", 0, low.astype(BF16)))
            terms.append(("im", 0, jnp.where(row < col, diag, 0.0).astype(BF16)))
        elif i == n - 1:
            terms.append(("either", n // 2, value))
        else:
            terms.append(("re" if i % 2 else "im", (i + 1) // 2, value))
    for at in range(0, half, step):

        def fields(d):
            rows = pl.ds(starts[d], tile)
            return green_ref[rows, at : at + step], green_ref[rows, half + at : half + at + step]

        yre, yim = jnp.zeros((tile, step), F32), jnp.zeros((tile, step), F32)
        for kind, d, value in terms:
            re, im = fields(d)
            tu, tv = along(value, re), along(value, im)
            if kind == "re":
                yre, yim = yre + tu, yim + tv
            elif kind == "im":
                yre, yim = yre - tv, yim + tu
            else:
                yre, yim = yre + jnp.where(real, tu, -tv), yim + jnp.where(real, tv, tu)
        re, im = fields(0)
        share = re.astype(F32) * yre + im.astype(F32) * yim
        emit(at, 2.0 * jnp.sum(share, axis=0, keepdims=True))


def sens_kernel(n, part, step, piece_ref, resid_ref, green_ref, out_ref):
    def emit(at, value):
        out_ref[:, at : at + step] = value

    sens_sum(n, part, step, piece_ref[0], resid_ref, green_ref, emit)


def last_kernel(n, part, step, piece_ref, column_ref, before_ref, resid_ref, green_ref, *out_refs):
    rows = out_refs[0].shape[0]
    column = column_ref[:, 0:1]

    def emit(at, value):
        product = column * (before_ref[:, at : at + step] + value)
        for k, out_ref in enumerate(out_refs):
            out_ref[:, at : at + step] = product[k * rows : (k + 1) * rows]

    sens_sum(n, part, step, piece_ref[0], resid_ref, green_ref, emit)


def first_sent(n):
    return n - 1, 0


SMEM = pl.BlockSpec(memory_space=pltpu.SMEM)
VMEM = pl.BlockSpec(memory_space=pltpu.VMEM)
HBM = pl.BlockSpec(memory_space=pltpu.HBM)


def call(kernel, shapes, specs, flops, moved, *args, scratch=(), alias={}, grant=24):
    out_shape = [jax.ShapeDtypeStruct(shape, dtype) for shape, dtype in shapes]
    out = pl.pallas_call(
        kernel,
        out_shape=out_shape,
        in_specs=specs,
        out_specs=[VMEM] * len(shapes),
        scratch_shapes=scratch,
        input_output_aliases=alias,
        compiler_params=pltpu.CompilerParams(vmem_limit_bytes=grant * MIB),
        cost_estimate=pl.CostEstimate(flops=flops, bytes_accessed=moved, transcendentals=0),
    )(*args)
    return out if len(out) > 1 else out[0]


def on_device(n_freq, n_cell, green, coeffs, basis, amplitude, block_mask):
    n = n_cell // 2
    bits, z_bits = n.bit_length() - 1, n_freq.bit_length() - 1
    stations, cells = green.shape[2], green.shape[3]
    tile, width, each = stations // n, 4 * cells, coeffs.shape[0]
    here = lax.axis_index("cell").astype(jnp.int32)
    plane = lax.axis_index("freq").astype(jnp.int32)
    core, chip = here % 2, here // 2
    flops = 2 * tile * tile * width
    moved = 2 * stations * width + 2 * tile * stations
    halves = [tuple(range(u * n // 2, (u + 1) * n // 2)) for u in (0, 1)]

    def dims(which):
        return [(which + j) % bits for j in range(bits)]

    swap_core = [(i, i ^ 1) for i in range(n_cell)]

    def swap_chip(value, j):
        pairs = [(i, i ^ (2 << dims(i % 2)[j])) for i in range(n_cell)]
        return lax.ppermute(value, "cell", pairs)

    def swap_plane(value, j):
        return lax.ppermute(value, "freq", [(i, i ^ (1 << j)) for i in range(n_freq)])

    def piece_of(q):
        flips = [sum(((q >> j) & 1) << dims(which)[j] for j in range(bits)) for which in (0, 1)]
        return chip ^ jnp.where(core == 0, flips[0], flips[1])

    cores, planes = core.reshape(1), plane.reshape(1)
    pieces = [piece_of(q).reshape(1) for q in range(n)]
    green = pltpu.with_memory_space_constraint(green, pltpu.HBM)
    two = [pltpu.SemaphoreType.DMA((2,))]
    theirs = call(
        take_kernel, [((2, stations, cells), BF16)], [SMEM, HBM] + [SMEM] * (n + 1), 0,
        8 * stations * cells, cores, green, planes, *pieces, scratch=two,
    )
    theirs = lax.ppermute(theirs, "cell", swap_core)
    known = coeffs
    for j in range(z_bits):
        near = swap_plane(known, j)
        known = jnp.concatenate((known, near), axis=0)
    beside = lax.ppermute(known, "cell", swap_core)
    known = jnp.concatenate((known, beside), axis=1)

    field = call(
        mine_kernel, [((stations, width), BF16)], [SMEM, HBM], 0,
        2 * stations * width, cores, green, scratch=two,
    )
    field, column = call(
        functools.partial(theirs_kernel, n_freq),
        [((stations, width), BF16), ((n_freq * each, 128), F32)], [SMEM, SMEM, SMEM, VMEM, VMEM], 0,
        2 * stations * width, cores, planes, basis, theirs, field, scratch=two, alias={4: 0},
    )

    def corr_parts(q, parts, dtype):
        shapes = [((tile, len(part) * tile), dtype) for part in parts]
        out = call(
            functools.partial(corr_kernel, n, parts), shapes, [SMEM, VMEM, VMEM, VMEM],
            flops * sum(len(part) for part in parts), moved, pieces[q], column, known, field,
        )
        return out if len(parts) > 1 else [out]

    held = {}
    for q in sorted(range(n), key=lambda q: (q % 2 == 0, -q)):
        if q % 2 == 0:
            held[q, 0], held[q, 1] = corr_parts(q, halves, F32)
            continue
        for u in (0, 1):
            if (q, u) == first_sent(n):
                middle = n // 4
                held[q, "b"] = corr_parts(q, [halves[u][middle:]], BF16)[0]
                held[q, "a"] = corr_parts(q, [halves[u][:middle]], BF16)[0]
            else:
                held[q, u] = corr_parts(q, [halves[u]], BF16)[0]
    weight = call(
        functools.partial(weight_kernel, n), [((tile, stations // 2), F32)] * 2,
        [SMEM, SMEM, VMEM, VMEM], 0, 4 * tile * stations, cores, pieces[0], amplitude, block_mask,
    )
    for j in range(bits):
        for q in sorted((q for q in range(n) if q % (1 << j) == 0 and (q >> j) & 1), reverse=True):
            for u in (0, 1):
                if (q, u) == first_sent(n):
                    late, early = (swap_chip(held[q, k], j) for k in "ab")
                    got = jnp.concatenate((late, early), axis=1)
                else:
                    got = swap_chip(held[q, u].astype(BF16), j)
                held[q ^ (1 << j), u] = held[q ^ (1 << j), u] + got.astype(F32)
    resid = {(0, u): (held[0, u] * weight[u]).astype(BF16) for u in (0, 1)}

    order, parts = [0], {"0": halves[0], "1": halves[1], "c": halves[1][: n // 4], "d": halves[1][n // 4 :]}
    cut = n // 4 * tile
    ends = {(0, "c"): resid[0, 1][:, :cut], (0, "d"): resid[0, 1][:, cut:]}
    for j in reversed(range(bits)):
        for q in list(order):
            order.append(q | (1 << j))
            for u in (0, 1):
                if u == 1 and order[-1] >= n // 2:
                    for k in "cd":
                        resid[order[-1], k] = swap_chip(ends[q, k], j)
                        ends[order[-1], k] = resid[order[-1], k]
                else:
                    resid[order[-1], u] = swap_chip(resid[q, u], j)
    step = min(512, width // 2)
    sens = 0.0
    for (q, u), value in resid.items():
        if (q, u) == (n - 1, "d"):
            continue
        part = parts[str(u)]
        sens = sens + call(
            functools.partial(sens_kernel, n, part, step), [((1, width // 2), F32)],
            [SMEM, VMEM, VMEM], flops * len(part), moved, pieces[q], value, field,
        )
    half_rows = ((n_freq * each // 2, width // 2), F32)
    low, high = call(
        functools.partial(last_kernel, n, parts["d"], step), [half_rows] * 2,
        [SMEM, VMEM, VMEM, VMEM, VMEM], flops * (n // 4), moved,
        pieces[n - 1], column, sens, resid[n - 1, "d"], field,
    )

    for j in reversed(range(z_bits)):
        kept = low + swap_plane(high, j)
        low, high = kept[: kept.shape[0] // 2], kept[kept.shape[0] // 2 :]
    return kept[:, :cells] + lax.ppermute(kept[:, cells:], "cell", swap_core)


def solution(mesh):
    placed = (
        P(None, "freq", None, "cell"),
        P("freq", "cell"),
        P("freq", None),
        P("freq", None),
        P(),
    )
    n_freq, n_cell = mesh.shape["freq"], mesh.shape["cell"]

    def body(*args):
        return on_device(n_freq, n_cell, *args)

    return jax.shard_map(
        body, mesh=mesh, in_specs=placed, out_specs=P("freq", "cell"), check_vma=False
    )
```

```python
import functools

import jax
import jax.numpy as jnp
from jax import lax
from jax.experimental import pallas as pl
from jax.experimental.pallas import tpu as pltpu
from jax.sharding import PartitionSpec as P


F32 = jnp.float32
BF16 = jnp.bfloat16
MIB = 1 << 20


def across(left, right):
    return lax.dot_general(left, right, (((1,), (1,)), ((), ())), preferred_element_type=F32)


def along(left, right):
    return jnp.dot(left, right, preferred_element_type=F32)


def start_all(sems, pairs):
    copies = [pltpu.make_async_copy(src, dst, sems.at[i]) for i, (src, dst) in enumerate(pairs)]
    for copy in copies:
        copy.start()
    return copies


def weight_kernel(n, core_ref, piece_ref, amp_ref, mask_ref, *weight_refs):
    core, piece = core_ref[0], piece_ref[0]
    tile = weight_refs[0].shape[0]
    blocks = mask_ref.shape[0]
    size = n * tile // blocks

    def amp(start):
        both = amp_ref[:, pl.ds(pl.multiple_of(start, tile), tile)]
        return jnp.where(core == 0, both[0:1], both[1:2])

    here = piece * tile
    row = lax.broadcasted_iota(jnp.int32, (tile, tile), 0)
    col = lax.broadcasted_iota(jnp.int32, (tile, tile), 1)
    down = jnp.sum(jnp.where(row == col, amp(here), 0.0), axis=1, keepdims=True)
    mask = mask_ref[...].astype(BF16)
    low = lax.broadcasted_iota(jnp.int32, (tile, blocks), 1) * size
    at = here + lax.broadcasted_iota(jnp.int32, (tile, blocks), 0)
    pick = ((at >= low) & (at < low + size)).astype(BF16)
    rows = (0.5 * (along(pick, mask) + across(pick, mask))).astype(BF16)
    low = lax.broadcasted_iota(jnp.int32, (blocks, tile), 0) * size
    for d in range(n // 2 + 1):
        start = lax.rem(piece + d, n) * tile
        at = start + lax.broadcasted_iota(jnp.int32, (blocks, tile), 1)
        pick = ((at >= low) & (at < low + size)).astype(BF16)
        weight = down * amp(start) * along(rows, pick)
        for i in [0] if d == 0 else [n - 1] if d == n // 2 else [2 * d - 1, 2 * d]:
            u = int(i >= split_at(n))
            at_block = i - u * split_at(n)
            weight_refs[u][:, at_block * tile : (at_block + 1) * tile] = weight


def take_kernel(core_ref, green_ref, *rest):
    out_ref, sems = rest[-2:]
    other = 1 - core_ref[0]
    for copy in start_all(sems, [(green_ref.at[p, other], out_ref.at[p]) for p in (0, 1)]):
        copy.wait()


def mine_kernel(core_ref, green_ref, out_ref, sems):
    core, cells = core_ref[0], green_ref.shape[3]
    spots = [out_ref.at[:, pl.ds(2 * p * cells, cells)] for p in (0, 1)]
    for copy in start_all(sems, [(green_ref.at[p, core], spots[p]) for p in (0, 1)]):
        copy.wait()


def theirs_kernel(planes, core_ref, plane_ref, basis_ref, theirs_ref, field_ref, out_ref, column_ref, sems):
    del field_ref
    core, plane, cells = core_ref[0], plane_ref[0], theirs_ref.shape[2]
    spots = [out_ref.at[:, pl.ds((2 * p + 1) * cells, cells)] for p in (0, 1)]
    copies = start_all(sems, [(theirs_ref.at[p], spots[p]) for p in (0, 1)])
    each = column_ref.shape[0] // planes
    at = lax.broadcasted_iota(jnp.int32, column_ref.shape, 0)
    column = jnp.zeros(column_ref.shape, F32)
    for i in range(column_ref.shape[0]):
        column = jnp.where(at == i, basis_ref[core, (plane ^ (i // each)) * each + i % each], column)
    column_ref[...] = column
    for copy in copies:
        copy.wait()


def corr_kernel(n, parts, piece_ref, column_ref, known_ref, green_ref, *out_refs):
    stations, width = green_ref.shape
    tile, half = stations // n, width // 2
    piece = piece_ref[0]

    def block(d):
        start = lax.rem(piece + d, n) * tile
        return green_ref[pl.ds(pl.multiple_of(start, tile), tile), :]

    def put(i, value):
        for part, out_ref in zip(parts, out_refs):
            if i in part:
                at = (i - part[0]) * tile
                out_ref[:, at : at + tile] = value.astype(out_ref.dtype)

    source = jnp.sum(column_ref[:, 0:1] * known_ref[...], axis=0, keepdims=True)
    source = jnp.concatenate((source, source), axis=1)
    scaled = (block(0).astype(F32) * source).astype(BF16)
    turned = jnp.concatenate((scaled[:, half:], -scaled[:, :half]), axis=1)
    both = jnp.concatenate((scaled, turned), axis=0)
    wanted = [i for part in parts for i in part]
    if 0 in wanted:
        pair = across(both, block(0))
        row = lax.broadcasted_iota(jnp.int32, (tile, tile), 0)
        col = lax.broadcasted_iota(jnp.int32, (tile, tile), 1)
        put(0, jnp.where(row >= col, pair[:tile], pair[tile:]))
    for d in range(1, n // 2):
        if 2 * d - 1 in wanted and 2 * d in wanted:
            pair = across(both, block(d))
            put(2 * d - 1, pair[:tile])
            put(2 * d, pair[tile:])
        elif 2 * d - 1 in wanted:
            put(2 * d - 1, across(scaled, block(d)))
        elif 2 * d in wanted:
            put(2 * d, across(turned, block(d)))
    if n - 1 in wanted:
        put(n - 1, across(jnp.where(piece < n // 2, scaled, turned), block(n // 2)))


def sens_sum(n, part, step, piece, resid_ref, green_ref, emit):
    stations, width = green_ref.shape
    tile, half = stations // n, width // 2
    starts = [pl.multiple_of(lax.rem(piece + d, n) * tile, tile) for d in range(n // 2 + 1)]
    real = piece < n // 2
    terms = []
    for i in part:
        at = (i - part[0]) * tile
        value = resid_ref[:, at : at + tile]
        if i == 0:
            row = lax.broadcasted_iota(jnp.int32, (tile, tile), 0)
            col = lax.broadcasted_iota(jnp.int32, (tile, tile), 1)
            diag = value.astype(F32)
            low = jnp.where(row > col, diag, jnp.where(row == col, 0.5 * diag, 0.0))
            terms.append(("re", 0, low.astype(BF16)))
            terms.append(("im", 0, jnp.where(row < col, diag, 0.0).astype(BF16)))
        elif i == n - 1:
            terms.append(("either", n // 2, value))
        else:
            terms.append(("re" if i % 2 else "im", (i + 1) // 2, value))
    for at in range(0, half, step):

        def fields(d):
            rows = pl.ds(starts[d], tile)
            return green_ref[rows, at : at + step], green_ref[rows, half + at : half + at + step]

        yre, yim = jnp.zeros((tile, step), F32), jnp.zeros((tile, step), F32)
        for kind, d, value in terms:
            re, im = fields(d)
            tu, tv = along(value, re), along(value, im)
            if kind == "re":
                yre, yim = yre + tu, yim + tv
            elif kind == "im":
                yre, yim = yre - tv, yim + tu
            else:
                yre, yim = yre + jnp.where(real, tu, -tv), yim + jnp.where(real, tv, tu)
        re, im = fields(0)
        share = re.astype(F32) * yre + im.astype(F32) * yim
        emit(at, 2.0 * jnp.sum(share, axis=0, keepdims=True))


def sens_kernel(n, part, step, piece_ref, resid_ref, green_ref, out_ref):
    def emit(at, value):
        out_ref[:, at : at + step] = value

    sens_sum(n, part, step, piece_ref[0], resid_ref, green_ref, emit)


def last_kernel(n, part, step, piece_ref, column_ref, before_ref, resid_ref, green_ref, *out_refs):
    rows = out_refs[0].shape[0]
    column = column_ref[:, 0:1]

    def emit(at, value):
        product = column * (before_ref[:, at : at + step] + value)
        for k, out_ref in enumerate(out_refs):
            out_ref[:, at : at + step] = product[k * rows : (k + 1) * rows]

    sens_sum(n, part, step, piece_ref[0], resid_ref, green_ref, emit)


def split_at(n):
    return n // 2


SMEM = pl.BlockSpec(memory_space=pltpu.SMEM)
VMEM = pl.BlockSpec(memory_space=pltpu.VMEM)
HBM = pl.BlockSpec(memory_space=pltpu.HBM)


def call(kernel, shapes, specs, flops, moved, *args, scratch=(), alias={}, grant=24):
    out_shape = [jax.ShapeDtypeStruct(shape, dtype) for shape, dtype in shapes]
    out = pl.pallas_call(
        kernel,
        out_shape=out_shape,
        in_specs=specs,
        out_specs=[VMEM] * len(shapes),
        scratch_shapes=scratch,
        input_output_aliases=alias,
        compiler_params=pltpu.CompilerParams(vmem_limit_bytes=grant * MIB),
        cost_estimate=pl.CostEstimate(flops=flops, bytes_accessed=moved, transcendentals=0),
    )(*args)
    return out if len(out) > 1 else out[0]


def on_device(n_freq, n_cell, green, coeffs, basis, amplitude, block_mask):
    n = n_cell // 2
    bits, z_bits = n.bit_length() - 1, n_freq.bit_length() - 1
    stations, cells = green.shape[2], green.shape[3]
    tile, width, each = stations // n, 4 * cells, coeffs.shape[0]
    here = lax.axis_index("cell").astype(jnp.int32)
    plane = lax.axis_index("freq").astype(jnp.int32)
    core, chip = here % 2, here // 2
    flops = 2 * tile * tile * width
    moved = 2 * stations * width + 2 * tile * stations
    halves = [tuple(range(split_at(n))), tuple(range(split_at(n), n))]

    def dims(which):
        return [(which + j) % bits for j in range(bits)]

    swap_core = [(i, i ^ 1) for i in range(n_cell)]

    def swap_chip(value, j):
        pairs = [(i, i ^ (2 << dims(i % 2)[j])) for i in range(n_cell)]
        return lax.ppermute(value, "cell", pairs)

    def swap_plane(value, j):
        return lax.ppermute(value, "freq", [(i, i ^ (1 << j)) for i in range(n_freq)])

    def piece_of(q):
        flips = [sum(((q >> j) & 1) << dims(which)[j] for j in range(bits)) for which in (0, 1)]
        return chip ^ jnp.where(core == 0, flips[0], flips[1])

    cores, planes = core.reshape(1), plane.reshape(1)
    pieces = [piece_of(q).reshape(1) for q in range(n)]
    green = pltpu.with_memory_space_constraint(green, pltpu.HBM)
    two = [pltpu.SemaphoreType.DMA((2,))]
    theirs = call(
        take_kernel, [((2, stations, cells), BF16)], [SMEM, HBM] + [SMEM] * (n + 1), 0,
        8 * stations * cells, cores, green, planes, *pieces, scratch=two,
    )
    theirs = lax.ppermute(theirs, "cell", swap_core)
    known = coeffs
    for j in range(z_bits):
        near = swap_plane(known, j)
        known = jnp.concatenate((known, near), axis=0)
    beside = lax.ppermute(known, "cell", swap_core)
    known = jnp.concatenate((known, beside), axis=1)

    field = call(
        mine_kernel, [((stations, width), BF16)], [SMEM, HBM], 0,
        2 * stations * width, cores, green, scratch=two,
    )
    field, column = call(
        functools.partial(theirs_kernel, n_freq),
        [((stations, width), BF16), ((n_freq * each, 128), F32)], [SMEM, SMEM, SMEM, VMEM, VMEM], 0,
        2 * stations * width, cores, planes, basis, theirs, field, scratch=two, alias={4: 0},
    )

    def corr_parts(q, parts, dtype):
        shapes = [((tile, len(part) * tile), dtype) for part in parts]
        out = call(
            functools.partial(corr_kernel, n, parts), shapes, [SMEM, VMEM, VMEM, VMEM],
            flops * sum(len(part) for part in parts), moved, pieces[q], column, known, field,
        )
        return out if len(parts) > 1 else [out]

    held = {}
    for q in sorted(range(n), key=lambda q: (q % 2 == 0, -q)):
        if q % 2 == 0:
            held[q, 0], held[q, 1] = corr_parts(q, halves, F32)
            continue
        for u in (0, 1):
            held[q, u] = corr_parts(q, [halves[u]], BF16)[0]
    weight = call(
        functools.partial(weight_kernel, n), [((tile, len(half) * tile), F32) for half in halves],
        [SMEM, SMEM, VMEM, VMEM], 0, 4 * tile * stations, cores, pieces[0], amplitude, block_mask,
    )
    for j in range(bits):
        for q in sorted((q for q in range(n) if q % (1 << j) == 0 and (q >> j) & 1), reverse=True):
            for u in (0, 1):
                got = swap_chip(held[q, u].astype(BF16), j)
                held[q ^ (1 << j), u] = held[q ^ (1 << j), u] + got.astype(F32)
    resid = {(0, u): (held[0, u] * weight[u]).astype(BF16) for u in (0, 1)}

    order = [0]
    for j in reversed(range(bits)):
        for q in list(order):
            order.append(q | (1 << j))
            for u in (0, 1):
                resid[order[-1], u] = swap_chip(resid[q, u], j)
    step = min(512, width // 2)
    sens = 0.0
    for (q, u), value in resid.items():
        if (q, u) == (n - 1, 1):
            continue
        part = halves[u]
        sens = sens + call(
            functools.partial(sens_kernel, n, part, step), [((1, width // 2), F32)],
            [SMEM, VMEM, VMEM], flops * len(part), moved, pieces[q], value, field,
        )
    half_rows = ((n_freq * each // 2, width // 2), F32)
    low, high = call(
        functools.partial(last_kernel, n, halves[1], step), [half_rows] * 2,
        [SMEM, VMEM, VMEM, VMEM, VMEM], flops * len(halves[1]), moved,
        pieces[n - 1], column, sens, resid[n - 1, 1], field,
    )

    for j in reversed(range(z_bits)):
        kept = low + swap_plane(high, j)
        low, high = kept[: kept.shape[0] // 2], kept[kept.shape[0] // 2 :]
    return kept[:, :cells] + lax.ppermute(kept[:, cells:], "cell", swap_core)


def solution(mesh):
    placed = (
        P(None, "freq", None, "cell"),
        P("freq", "cell"),
        P("freq", None),
        P("freq", None),
        P(),
    )
    n_freq, n_cell = mesh.shape["freq"], mesh.shape["cell"]

    def body(*args):
        return on_device(n_freq, n_cell, *args)

    return jax.shard_map(
        body, mesh=mesh, in_specs=placed, out_specs=P("freq", "cell"), check_vma=False
    )
```
